128 devices in a mesh: cam: 8 (over z, core), ray: 16 (over y, x).
Axes of the slice: x: 4, y: 4, z: 4, core: 2. Of those that a mesh axis runs over, the one named last changes fastest.
Arguments:
- encodings: bfloat16 [8192, 48, 128], P(('cam', 'ray')), may hold values from -6 to 6
- ray_camera: int32 [8192], P(('cam', 'ray')), may hold values from 0 to 32767, as said below
- targets: float32 [8192, 3], P(('cam', 'ray')), may hold values from -6 to 6
- weights: bfloat16 [4, 128, 128], replicated, may hold values from -0.5 to 0.5
- head_weight: bfloat16 [128, 3], replicated, may hold values from -0.5 to 0.5
- quadrature: float32 [48], replicated, may hold values from 0.05 to 0.3
- lift: float32 [38, 128], replicated, may hold values from -1 to 1
- cam_params: float32 [38, 32768], P(None, ('cam', 'ray')), may hold values from -6 to 6
- damping: float32 [38, 32768], P(None, ('cam', 'ray')), may hold values from 1 to 30
Outputs:
- update: float32 [38, 32768], P(None, ('cam', 'ray'))
- cg_residual: float32 [38, 32768], P(None, ('cam', 'ray'))
The draws below stay inside these ranges and needn't reach their ends.
Inputs may be any that keep to these rules, and one draw needn't show every extreme that they name: ray_camera is the same for all 64 rays of each aligned block of 64 rays.
All inputs are finite; a program needn't handle non-finite values.
Results may differ from the reference program's by a relative error of at most 0.008.
Values sent between devices are 32-bit elements; how exact they have to be, the bound alone decides.
A program may use at most 64 MiB of HBM per device.

```python
import math
import jax
import jax.numpy as jnp
from jax import lax

D = 128
LAYERS = 4
SAMPLES = 48
COLORS = 3
BLOCK = 64
CG_ITERS = 2
RAY_DEV = 64
PARAMS = 38
OWNERS = 128
CAMERAS = 32768
RAYS = 8192
BLOCKS = 128


def draw_ray_camera(key, part):
    cameras = jax.random.randint(jax.random.fold_in(key, 17), (BLOCKS,), 0, CAMERAS, dtype=jnp.int32)
    return jnp.repeat(cameras, BLOCK, total_repeat_length=RAYS)


def block_scale(rng, extent, shards, least, top_value):
    def one(axis_at, shards_of):
        draws = jax.random.uniform(jax.random.fold_in(jax.random.fold_in(rng, 6), axis_at), (shards_of,), jnp.float32, least / len(shards), top_value / len(shards))
        return jnp.repeat(jnp.exp(draws), extent[axis_at] // shards_of).reshape((-1,) + (1,) * (len(extent) - axis_at - 1))

    loudness = one(*shards[0])
    for cut in shards[1:]:
        loudness = loudness * one(*cut)
    return loudness


def gaussian(own_key, dims, width, limit, pieces=(), held_as=jnp.bfloat16):
    gain = block_scale(own_key, dims, pieces, -0.22, 0.18) if pieces else 1.0
    drawn = jax.random.normal(own_key, dims, jnp.float32) * width * gain
    return jnp.minimum(jnp.maximum(drawn, -limit), limit).astype(held_as)


def setup_inputs(seed: int = 0) -> dict:
    streams_of = jax.random.split(jax.random.key(seed), 10)
    return {
        "encodings": gaussian(streams_of[0], (RAYS, SAMPLES, D), 1.0, 6.0, ((0, 128),)),
        "ray_camera": draw_ray_camera(jax.random.fold_in(streams_of[9], 71), 0),
        "targets": gaussian(streams_of[2], (RAYS, COLORS), 1.0, 6.0, ((0, 128),), jnp.float32),
        "weights": gaussian(streams_of[3], (LAYERS, D, D), D ** -0.5, 0.5),
        "head_weight": gaussian(streams_of[4], (D, COLORS), D ** -0.5, 0.5),
        "quadrature": jnp.clip(jnp.exp(jax.random.uniform(streams_of[5], (SAMPLES,), jnp.float32, math.log(0.05), math.log(0.3))), 0.05, 0.3),
        "lift": gaussian(streams_of[6], (PARAMS, D), PARAMS ** -0.5, 1.0, (), jnp.float32),
        "cam_params": gaussian(streams_of[7], (PARAMS, CAMERAS), 1.0, 6.0, ((1, 128),), jnp.float32),
        "damping": jnp.clip(jnp.exp(math.log(30.0) - 3.4011974 * jax.random.uniform(streams_of[8], (PARAMS, CAMERAS), jnp.float32) ** block_scale(streams_of[8], (PARAMS, CAMERAS), ((1, 128),), -0.2, 0.2)), 1.0, 30.0),
    }


precise = lax.Precision.HIGHEST


def forward(enc_group, lifted, weights, depths):
    row_count, sample_count, feature_width = enc_group.shape
    inner = enc_group.astype(jnp.float32) + depths[None, :, None] * lifted[:, None, :]
    layer_out = jnp.tanh(inner).astype(jnp.bfloat16)
    outputs = [layer_out]
    for layer in range(weights.shape[0]):
        inner = jnp.dot(layer_out.reshape(row_count * sample_count, feature_width), weights[layer], preferred_element_type=jnp.float32)
        layer_out = jnp.tanh(inner).astype(jnp.bfloat16).reshape(row_count, sample_count, feature_width)
        outputs.append(layer_out)
    return outputs


def render(layer_out, head_weight, quadrature):
    mixed = jnp.sum(quadrature[None, :, None] * layer_out.astype(jnp.float32), axis=1)
    return jnp.dot(mixed, head_weight.astype(jnp.float32), precision=precise)


def tangent_pass(outputs, spread, weights, head_weight, quadrature, depths):
    row_count, sample_count, feature_width = outputs[0].shape
    slope = 1.0 - outputs[0].astype(jnp.float32) ** 2
    tangent = (slope * depths[None, :, None] * spread[:, None, :]).astype(jnp.bfloat16)
    for layer in range(weights.shape[0]):
        inner = jnp.dot(tangent.reshape(row_count * sample_count, feature_width), weights[layer], preferred_element_type=jnp.float32)
        slope = 1.0 - outputs[layer + 1].astype(jnp.float32) ** 2
        tangent = (slope * inner.reshape(row_count, sample_count, feature_width)).astype(jnp.bfloat16)
    return render(tangent, head_weight, quadrature)


def adjoint_pass(outputs, pixel_grad, weights, head_weight, quadrature, depths):
    row_count, sample_count, feature_width = outputs[0].shape
    cotangent = jnp.dot(pixel_grad, head_weight.astype(jnp.float32).T, precision=precise)
    slope = 1.0 - outputs[-1].astype(jnp.float32) ** 2
    adjoint = (slope * quadrature[None, :, None] * cotangent[:, None, :]).astype(jnp.bfloat16)
    for layer in reversed(range(weights.shape[0])):
        inner = jnp.dot(adjoint.reshape(row_count * sample_count, feature_width), weights[layer].T, preferred_element_type=jnp.float32)
        slope = 1.0 - outputs[layer].astype(jnp.float32) ** 2
        adjoint = (slope * inner.reshape(row_count, sample_count, feature_width)).astype(jnp.bfloat16)
    return jnp.sum(depths[None, :, None] * adjoint.astype(jnp.float32), axis=1)


def reference(encodings, ray_camera, targets, weights, head_weight, quadrature, lift, cam_params, damping):
    depths = (jnp.arange(SAMPLES).astype(jnp.float32) + 1.0) / SAMPLES
    block_cam = ray_camera.reshape(BLOCKS, BLOCK)[:, 0]

    def spread_rays(values):
        lifted = jnp.dot(lift.T, values[:, block_cam], precision=precise)
        return jnp.repeat(lifted.T, BLOCK, axis=0).reshape(OWNERS, RAY_DEV, D)

    def sum_to_cameras(ray_grads):
        summed = ray_grads.reshape(BLOCKS, BLOCK, D).sum(axis=1)
        grads = jnp.dot(lift, summed.T, precision=precise)
        return jnp.zeros((PARAMS, CAMERAS), jnp.float32).at[:, block_cam].add(grads)

    lifted_all = spread_rays(cam_params)
    enc_groups = encodings.reshape(OWNERS, RAY_DEV, SAMPLES, D)
    target_groups = targets.reshape(OWNERS, RAY_DEV, COLORS)

    def initial(group_item):
        enc_group, lifted, target_group = group_item
        outputs = forward(enc_group, lifted, weights, depths)
        residual_rays = render(outputs[-1], head_weight, quadrature) - target_group
        return adjoint_pass(outputs, residual_rays, weights, head_weight, quadrature, depths)

    right_side = -sum_to_cameras(lax.map(initial, (enc_groups, lifted_all, target_groups)))

    def operator(vector):
        spread_all = spread_rays(vector)

        def single_group(group_item):
            enc_group, lifted, spread = group_item
            outputs = forward(enc_group, lifted, weights, depths)
            image_rays = tangent_pass(outputs, spread, weights, head_weight, quadrature, depths)
            return adjoint_pass(outputs, image_rays, weights, head_weight, quadrature, depths)

        return sum_to_cameras(lax.map(single_group, (enc_groups, lifted_all, spread_all))) + damping * vector

    solution = jnp.zeros((PARAMS, CAMERAS), jnp.float32)
    remainder = right_side
    direction = right_side
    norm_now = jnp.sum(remainder * remainder)
    for step_index in range(CG_ITERS):
        image = operator(direction)
        step_size = norm_now / jnp.sum(direction * image)
        solution = solution + step_size * direction
        remainder = remainder - step_size * image
        if step_index + 1 < CG_ITERS:
            norm_next = jnp.sum(remainder * remainder)
            direction = remainder + (norm_next / norm_now) * direction
            norm_now = norm_next
    return solution, remainder
```

```python
import functools

import jax
import jax.numpy as jnp
from jax import lax
from jax.experimental import pallas as pl
from jax.experimental.pallas import tpu as pltpu
from jax.sharding import PartitionSpec as P

F = jnp.float32
B = jnp.bfloat16
MESH = pl.DeviceIdType.MESH
BOTH = ("cam", "ray")
N = 128
D = 128
SAMPLES = 48
COLORS = 3
RAYS = 64
LAYERS = 4
PARAMS = 38
COLS = 256
CG_ITERS = 2
STEP_RAYS = 32
HI = lax.Precision.HIGHEST
OFFS = (0, 40, 72, 96, 112)


def hops(d):
    return min(d, 4 - d)


OTHERS = sorted(
    (
        (dz, dc, dy, dx)
        for dz in range(4)
        for dc in range(2)
        for dy in range(4)
        for dx in range(4)
        if (dz, dc, dy, dx) != (0, 0, 0, 0)
    ),
    key=lambda o: -(hops(o[0]) + hops(o[2]) + hops(o[3])),
)


def partners():
    cam, ray = lax.axis_index("cam"), lax.axis_index("ray")
    z, c, y, x = cam // 2, cam % 2, ray // 4, ray % 4
    zs = [(z + d) % 4 * 2 for d in range(4)]
    cs = [(c + d) % 2 for d in range(2)]
    ys = [(y + d) % 4 * 4 for d in range(4)]
    xs = [(x + d) % 4 for d in range(4)]
    cams = {(dz, dc): zs[dz] + cs[dc] for dz in range(4) for dc in range(2)}
    rays = {(dy, dx): ys[dy] + xs[dx] for dy in range(4) for dx in range(4)}
    return cam * 16 + ray, [(cams[o[:2]], rays[o[2:]]) for o in OTHERS]


def dot(a, b, dims, precision=HI):
    return lax.dot_general(a, b, (dims, ((), ())), precision=precision, preferred_element_type=F)


def mlp(enc, de, w, wt, hw, quad, depth, grads, mixed):
    rows = STEP_RAYS * SAMPLES
    quad, depth = quad[None], depth[None]

    def step(t, carry):
        at = pl.ds(pl.multiple_of(t * STEP_RAYS, STEP_RAYS), STEP_RAYS)
        h = jnp.tanh(enc[at].astype(F) + de[None]).astype(B).reshape(rows, D)
        hs = [h]
        for layer in range(LAYERS):
            h = jnp.tanh(jnp.dot(h, w[layer], preferred_element_type=F)).astype(B)
            hs.append(h)
        last = h.astype(F).reshape(STEP_RAYS, SAMPLES, D)
        mixed[at] = jnp.sum(quad * last, axis=1)
        slope = ((1.0 - last * last) * quad).reshape(rows, D)
        ys = [(slope * hw[c : c + 1]).astype(B) for c in range(COLORS)]
        for layer in range(LAYERS - 1, 0, -1):
            inner = hs[layer].astype(F)
            slope = 1.0 - inner * inner
            ys = [(jnp.dot(y, wt[layer], preferred_element_type=F) * slope).astype(B) for y in ys]
        first = hs[0].astype(F).reshape(STEP_RAYS, SAMPLES, D)
        slope = (1.0 - first * first) * depth
        for c in range(COLORS):
            inner = jnp.dot(ys[c], wt[0], preferred_element_type=F)
            grads[c, at] = jnp.sum(inner.reshape(STEP_RAYS, SAMPLES, D) * slope, axis=1)
        return carry

    lax.fori_loop(0, RAYS // STEP_RAYS, step, 0)


def matvec(tiles, v):
    sub = lax.broadcasted_iota(jnp.int32, (8, N), 0)
    outs = [jnp.zeros((8, N), F) for _ in range(5)]
    for r in range(8):
        for a in range(5):
            if 8 * a + r >= PARAMS:
                continue
            own = v[a][r : r + 1]
            total = None
            for j in range(a, 5):
                at = OFFS[a] + 8 * (j - a)
                piece = tiles[r, at : at + 8]
                term = piece * v[j]
                total = term if total is None else total + term
                if j > a:
                    outs[j] = outs[j] + piece * own
            row = jnp.sum(total, axis=0, keepdims=True)
            outs[a] = outs[a] + jnp.where(sub == r, row, 0.0)
    return outs


def kernel(
    ids_in, quad_in, enc_in, targets_in, w_in, hw_in, lift_in, params_in, damping_in,
    update_out, residual_out,
    enc, owned, lift, wt, quad, id_row, ids, reply, columns, grads, mixed, tile, tiles, turned,
    local_sem, send_sem, recv_sem,
):
    me, others = partners()

    def exchange(n, source, target):
        for p in others:
            pltpu.make_async_remote_copy(
                source(p), target.at[me], send_sem.at[n], recv_sem.at[n],
                device_id=p, device_id_type=MESH,
            ).start()

    def landed(n, target):
        all_others = target.at[pl.ds(0, N - 1)]
        pltpu.make_async_copy(all_others, all_others, recv_sem.at[n]).wait()

    def sent(n, target):
        all_others = target.at[pl.ds(0, N - 1)]
        pltpu.make_async_copy(all_others, all_others, send_sem.at[n]).wait()

    barrier = pltpu.get_barrier_semaphore()
    for p in others:
        pl.semaphore_signal(barrier, inc=1, device_id=p, device_id_type=MESH)
    load = pltpu.make_async_copy(enc_in, enc, local_sem.at[0])
    load.start()

    id_row[0] = jnp.full((8, D), ids_in[0].astype(F), F)
    owned[...] = jnp.zeros_like(owned)
    owned[0:PARAMS] = params_in[...]
    owned[40 : 40 + PARAMS] = damping_in[...]
    lift[...] = jnp.zeros_like(lift)
    lift[0:PARAMS] = lift_in[...]
    for layer in range(LAYERS):
        wt[layer] = w_in[layer].T
    for s in range(SAMPLES):
        quad[s : s + 1] = jnp.full((1, D), quad_in[s], F)
    depth = (lax.broadcasted_iota(jnp.int32, (SAMPLES, D), 0).astype(F) + 1.0) / SAMPLES
    hw = hw_in[...].astype(F)
    pl.semaphore_wait(barrier, N - 1)

    exchange(0, lambda p: id_row.at[0, pl.ds(0, 1)], ids)
    ids[me] = id_row[0, 0:1]
    landed(0, ids)
    lane = lax.broadcasted_iota(jnp.int32, (N, D), 1).astype(F)
    base = (me * COLS).astype(F)
    asked = ids[...].reshape(N, D) - base
    picked = jnp.concatenate(
        [(asked == lane).astype(F), (asked == lane + 128.0).astype(F)], axis=1
    )
    reply[...] = dot(picked, owned[...], ((1,), (1,))).reshape(N, 1, D)
    exchange(1, lambda p: reply.at[p[0] * 16 + p[1]], columns)
    columns[me] = reply[me]
    landed(1, columns)
    column = jnp.sum(columns[...].reshape(N, D), axis=0, keepdims=True)
    lifted = dot(jnp.broadcast_to(column, (8, D)), lift[...], ((1,), (0,)))[0:1]
    load.wait()
    mlp(enc, depth * lifted, w_in, wt, hw, quad[...], depth, grads, mixed)

    residual = dot(hw, mixed[...], ((1,), (1,))) - targets_in[...]
    lane8 = lax.broadcasted_iota(jnp.int32, (8, D), 1)
    sub8 = lax.broadcasted_iota(jnp.int32, (8, D), 0)
    rows = dot(grads[...].reshape(COLORS * RAYS, D), lift[...], ((1,), (1,)))
    matrix = dot(rows.T[0:40], rows, ((1,), (0,)))
    right = jnp.zeros((1, D), F)
    for c in range(COLORS):
        part = rows[c * RAYS : (c + 1) * RAYS]
        right = right - dot(residual[c : c + 1], part, ((1,), (0,)))
    right = jnp.broadcast_to(right, (8, D))
    damp = pltpu.roll(jnp.broadcast_to(column, (8, D)), D - 40, axis=1)
    damp = jnp.where(lane8 == PARAMS, id_row[0], damp)
    out = jnp.zeros((8, D), F)
    for a in range(5):
        moved = matrix[8 * a : 8 * a + 8]
        if a:
            moved = pltpu.roll(moved, OFFS[a] - 8 * a, axis=1)
        inside = (lane8 >= OFFS[a]) & (lane8 < OFFS[a] + 40 - 8 * a)
        out = jnp.where(inside, moved, out)
    for value, sub, first, start in (
        [(right, m, 8 * m, 120) for m in range(5)]
        + [(damp, 5 + m, 8 * m, 120) for m in range(3)]
        + [(damp, 6, 24, 112), (damp, 7, 32, 112)]
    ):
        moved = pltpu.roll(value, start - first, axis=1)
        inside = (sub8 == sub) & (lane8 >= start) & (lane8 < start + 8)
        out = jnp.where(inside, moved, out)
    tile[0] = out
    exchange(2, lambda p: tile.at[0], tiles)
    tiles[me] = tile[0]
    landed(2, tiles)

    for r in range(8):
        turned[r] = tiles[:, r, :].T
    rhs = jnp.concatenate([turned[m, 120:128] for m in range(5)], axis=0)
    damping = jnp.concatenate(
        [turned[5, 120:128], turned[6, 120:128], turned[7, 120:128], turned[6, 112:120],
         turned[7, 112:120]], axis=0,
    )
    id_lanes = damping[PARAMS : PARAMS + 1]
    row40 = lax.broadcasted_iota(jnp.int32, (40, N), 0)
    damping = jnp.where(row40 < PARAMS, damping, 0.0)
    id_subs = tiles[:, 7, 112 + 6 : 112 + 7]
    same = id_subs == id_lanes
    earlier = lax.broadcasted_iota(jnp.int32, (N, N), 0) < lax.broadcasted_iota(jnp.int32, (N, N), 1)
    repeats = jnp.sum(jnp.where(same & earlier, 1.0, 0.0), axis=0, keepdims=True)
    once = jnp.where(repeats == 0.0, 1.0, 0.0)
    same = same.astype(F)

    def total(v):
        return jnp.sum(jnp.sum(v * once, axis=0, keepdims=True), axis=1, keepdims=True)

    def operator(v):
        product = matvec(turned, [v[8 * a : 8 * a + 8] for a in range(5)])
        return dot(jnp.concatenate(product, axis=0), same, ((1,), (0,))) + damping * v

    remainder = dot(rhs, same, ((1,), (0,)))
    direction = remainder
    norm = total(remainder * remainder)
    answer = jnp.zeros_like(remainder)
    for it in range(CG_ITERS):
        image = operator(direction)
        step = norm / total(direction * image)
        answer = answer + step * direction
        remainder = remainder - step * image
        if it + 1 < CG_ITERS:
            norm_next = total(remainder * remainder)
            direction = remainder + (norm_next / norm) * direction
            norm = norm_next
    mine = id_subs - base
    wide = lax.broadcasted_iota(jnp.int32, (N, COLS), 1).astype(F)
    place = (mine == wide).astype(F)
    update_out[...] = dot(answer * once, place, ((1,), (0,)))[0:PARAMS]
    residual_out[...] = dot(remainder * once, place, ((1,), (0,)))[0:PARAMS]
    sent(0, ids)
    sent(1, columns)
    sent(2, tiles)


def body(encodings, ray_camera, targets, weights, head_weight, quadrature, lift, cam_params, damping):
    vmem = pl.BlockSpec(memory_space=pltpu.VMEM)
    smem = pl.BlockSpec(memory_space=pltpu.SMEM)
    out = jax.ShapeDtypeStruct((PARAMS, COLS), F)
    return pl.pallas_call(
        kernel,
        out_shape=(out, out),
        in_specs=[smem, smem, pl.BlockSpec(memory_space=pl.ANY)] + [vmem] * 6,
        out_specs=(vmem, vmem),
        scratch_shapes=[
            pltpu.VMEM((RAYS, SAMPLES, D), B),
            pltpu.VMEM((D, COLS), F),
            pltpu.VMEM((D, D), F),
            pltpu.VMEM((LAYERS, D, D), B),
            pltpu.VMEM((SAMPLES, D), F),
            pltpu.VMEM((1, 8, D), F),
            pltpu.VMEM((N, 1, D), F),
            pltpu.VMEM((N, 1, D), F),
            pltpu.VMEM((N, 1, D), F),
            pltpu.VMEM((COLORS, RAYS, D), F),
            pltpu.VMEM((RAYS, D), F),
            pltpu.VMEM((1, 8, D), F),
            pltpu.VMEM((N, 8, D), F),
            pltpu.VMEM((8, D, N), F),
            pltpu.SemaphoreType.DMA((1,)),
            pltpu.SemaphoreType.DMA((3,)),
            pltpu.SemaphoreType.DMA((3,)),
        ],
        name="pose_update",
        compiler_params=pltpu.CompilerParams(
            collective_id=0, has_side_effects=True, vmem_limit_bytes=60 * 2**20
        ),
    )(ray_camera, quadrature, encodings, targets.T, weights, head_weight.T, lift, cam_params, damping)


def solution(mesh):
    in_specs = (
        P(BOTH, None, None), P(BOTH), P(BOTH, None), P(), P(), P(), P(), P(None, BOTH), P(None, BOTH),
    )
    out_specs = (P(None, BOTH), P(None, BOTH))
    return jax.shard_map(body, mesh=mesh, in_specs=in_specs, out_specs=out_specs, check_vma=False)
```

```python
import functools

import jax
import jax.numpy as jnp
from jax import lax
from jax.experimental import pallas as pl
from jax.experimental.pallas import tpu as pltpu
from jax.sharding import PartitionSpec as P

F = jnp.float32
B = jnp.bfloat16
MESH = pl.DeviceIdType.MESH
BOTH = ("cam", "ray")
N = 128
D = 128
SAMPLES = 48
COLORS = 3
RAYS = 64
LAYERS = 4
PARAMS = 38
COLS = 256
CG_ITERS = 2
STEP_RAYS = 32
HI = lax.Precision.HIGHEST
OFFS = (0, 40, 72, 96, 112)


def far(o):
    return sum(min(d, 4 - d) for d in (o[0], o[2], o[3]))


OTHERS = sorted(
    (
        (dz, dc, dy, dx)
        for dz in range(4)
        for dc in range(2)
        for dy in range(4)
        for dx in range(4)
        if (dz, dc, dy, dx) != (0, 0, 0, 0)
    ),
    key=lambda o: -far(o),
)
PLANE = [o for o in OTHERS if o[3] == 0]
LINE = [o for o in OTHERS if o[:3] == (0, 0, 0)]
SAME = [o for o in OTHERS if o[1] == 0]
PAIR = (0, 1, 0, 0)
ASKERS = len(PLANE) + 1
HALF = len(SAME) + 1
GROUPS = [[i for i, o in enumerate(SAME) if far(o) in hops] for hops in ((1, 2), (3,), (4, 5, 6))]


def device(o):
    cam, ray = lax.axis_index("cam"), lax.axis_index("ray")
    z, c, y, x = cam // 2, cam % 2, ray // 4, ray % 4
    return (z + o[0]) % 4 * 2 + (c + o[1]) % 2, (y + o[2]) % 4 * 4 + (x + o[3]) % 4


def opposite(o):
    return (-o[0]) % 4, (-o[1]) % 2, (-o[2]) % 4, (-o[3]) % 4


def dot(a, b, dims, precision=HI):
    return lax.dot_general(a, b, (dims, ((), ())), precision=precision, preferred_element_type=F)


def dot_ones(a, b, dims):
    high = a.astype(B)
    rest = a - high.astype(F)
    middle = rest.astype(B)
    low = (rest - middle.astype(F)).astype(B)
    n = a.shape[0]
    out = dot(jnp.concatenate([high, middle, low], axis=0), b, dims, None)
    return out[0:n] + out[n : 2 * n] + out[2 * n : 3 * n]


def mlp(enc, de, w, wt, hw, quad, depth, grads, mixed):
    rows = STEP_RAYS * SAMPLES
    quad, depth = quad[None], depth[None]

    def step(t, carry):
        at = pl.ds(pl.multiple_of(t * STEP_RAYS, STEP_RAYS), STEP_RAYS)
        h = jnp.tanh(enc[at].astype(F) + de[None]).astype(B).reshape(rows, D)
        hs = [h]
        for layer in range(LAYERS):
            h = jnp.tanh(jnp.dot(h, w[layer], preferred_element_type=F)).astype(B)
            hs.append(h)
        last = h.astype(F).reshape(STEP_RAYS, SAMPLES, D)
        mixed[at] = jnp.sum(quad * last, axis=1)
        slope = ((1.0 - last * last) * quad).reshape(rows, D)
        ys = [(slope * hw[c : c + 1]).astype(B) for c in range(COLORS)]
        for layer in range(LAYERS - 1, 0, -1):
            inner = hs[layer].astype(F)
            slope = 1.0 - inner * inner
            ys = [(jnp.dot(y, wt[layer], preferred_element_type=F) * slope).astype(B) for y in ys]
        first = hs[0].astype(F).reshape(STEP_RAYS, SAMPLES, D)
        slope = (1.0 - first * first) * depth
        for c in range(COLORS):
            inner = jnp.dot(ys[c], wt[0], preferred_element_type=F)
            grads[c, at] = jnp.sum(inner.reshape(STEP_RAYS, SAMPLES, D) * slope, axis=1)
        return carry

    lax.fori_loop(0, RAYS // STEP_RAYS, step, 0)


def matvec(turned, v):
    sub = lax.broadcasted_iota(jnp.int32, (8, N), 0)
    outs = [jnp.zeros((8, N), F) for _ in range(5)]
    for r in range(8):
        for a in range(5):
            if 8 * a + r >= PARAMS:
                continue
            own = v[a][r : r + 1]
            total = None
            for j in range(a, 5):
                at = OFFS[a] + 8 * (j - a)
                piece = turned[r, at : at + 8]
                term = piece * v[j]
                total = term if total is None else total + term
                if j > a:
                    outs[j] = outs[j] + piece * own
            row = jnp.sum(total, axis=0, keepdims=True)
            outs[a] = outs[a] + jnp.where(sub == r, row, 0.0)
    return outs


def kernel(
    quad_in, ids_in, enc_in, targets_in, w_in, hw_in, lift_in, params_in, damping_in,
    result_out,
    enc, targets, w, hw_b, lift_b, wt, lift, quad, ids, owned, owned_damping,
    reply, reply_damping, columns, columns_damping, grads, mixed, tiles, turned,
    load_sem, send_sem, recv_sem, group_sem,
):
    def send(source, target, n, o, recv=None):
        pltpu.make_async_remote_copy(
            source, target, send_sem.at[n], recv_sem.at[n] if recv is None else recv,
            device_id=device(o), device_id_type=MESH,
        ).start()

    def wait(ref, sem):
        pltpu.make_async_copy(ref, ref, sem).wait()

    barrier = pltpu.get_barrier_semaphore()
    for o in PLANE + LINE:
        pl.semaphore_signal(barrier, inc=1, device_id=device(o), device_id_type=MESH)
    loads = [
        pltpu.make_async_copy(source, target, load_sem.at[i])
        for i, (source, target) in enumerate(
            [
                (ids_in, ids.at[ASKERS - 1]),
                (params_in, owned.at[0]),
                (damping_in, owned_damping.at[0]),
                (lift_in, lift_b),
                (w_in, w),
                (hw_in, hw_b),
                (targets_in, targets),
                (enc_in, enc),
            ]
        )
    ]
    for load in loads:
        load.start()

    reply[...] = jnp.zeros_like(reply)
    reply_damping[...] = jnp.zeros_like(reply_damping)
    lift[...] = jnp.zeros_like(lift)
    for s in range(SAMPLES):
        quad[s : s + 1] = jnp.full((1, D), quad_in[s], F)
    depth = (lax.broadcasted_iota(jnp.int32, (SAMPLES, D), 0).astype(F) + 1.0) / SAMPLES
    loads[0].wait()
    loads[1].wait()
    pl.semaphore_wait(barrier, len(PLANE) + len(LINE))

    for o in LINE:
        send(owned.at[0], owned.at[o[3]], 1, o)
    for i, o in enumerate(PLANE):
        send(ids.at[ASKERS - 1], ids.at[i], 0, o)
    loads[2].wait()
    for o in LINE:
        send(owned_damping.at[0], owned_damping.at[o[3]], 2, o)
    for load in loads[3:7]:
        load.wait()
    lift[0:PARAMS] = lift_b[...]
    for layer in range(LAYERS):
        wt[layer] = w[layer].T
    hw = hw_b[...].astype(F)
    wait(ids.at[pl.ds(0, ASKERS - 1)], recv_sem.at[0])

    asked = ids[...].reshape(ASKERS, RAYS).astype(F)
    here = lax.broadcasted_iota(jnp.int32, (ASKERS, RAYS), 0) == lax.broadcasted_iota(
        jnp.int32, (ASKERS, RAYS), 1
    )
    asked = jnp.sum(jnp.where(here, asked, 0.0), axis=0, keepdims=True)
    count = lax.broadcasted_iota(jnp.int32, (COLS, RAYS), 0).astype(F)
    picked = []
    for t in range(4):
        cam, ray = device((0, 0, 0, (4 - t) % 4))
        first = ((cam * 16 + ray) * COLS).astype(F)
        picked.append((asked - first == count).astype(B))
    picked = jnp.concatenate(picked, axis=0)

    def answer(held, rows, landing, n):
        wide = jnp.concatenate([held[t] for t in range(4)], axis=1)
        wide = jnp.concatenate([wide, jnp.zeros((2, 4 * COLS), F)], axis=0)
        got = dot_ones(wide, picked, ((1,), (0,)))
        rows[:, 0, 0:40] = got.T[0:ASKERS]
        for i, o in enumerate(PLANE):
            send(rows.at[i], landing.at[i], n, opposite(o))
        landing[ASKERS - 1] = rows[ASKERS - 1]

    wait(owned.at[pl.ds(1, 3)], recv_sem.at[1])
    answer(owned, reply, columns, 3)
    wait(owned_damping.at[pl.ds(1, 3)], recv_sem.at[2])
    answer(owned_damping, reply_damping, columns_damping, 4)
    wait(columns.at[pl.ds(0, ASKERS - 1)], recv_sem.at[3])
    column = jnp.sum(columns[...].reshape(ASKERS, D), axis=0, keepdims=True)
    lifted = dot(jnp.broadcast_to(column, (8, D)), lift[...], ((1,), (0,)))[0:1]
    loads[7].wait()
    mlp(enc, depth * lifted, w, wt, hw, quad[...], depth, grads, mixed)

    wait(columns_damping.at[pl.ds(0, ASKERS - 1)], recv_sem.at[4])
    damp = jnp.sum(columns_damping[...].reshape(ASKERS, D), axis=0, keepdims=True)
    residual = dot(hw, mixed[...], ((1,), (1,))) - targets[...]
    lane8 = lax.broadcasted_iota(jnp.int32, (8, D), 1)
    sub8 = lax.broadcasted_iota(jnp.int32, (8, D), 0)
    rows = dot(grads[...].reshape(COLORS * RAYS, D), lift[...], ((1,), (1,)))
    matrix = dot(rows.T[0:40], rows, ((1,), (0,)))
    right = jnp.zeros((1, D), F)
    for c in range(COLORS):
        part = rows[c * RAYS : (c + 1) * RAYS]
        right = right - dot(residual[c : c + 1], part, ((1,), (0,)))
    right = jnp.broadcast_to(right, (8, D))
    camera = ids[ASKERS - 1][:, 0:1].astype(F)
    damp = jnp.where(lane8 == PARAMS, camera, jnp.broadcast_to(damp, (8, D)))
    out = jnp.zeros((8, D), F)
    for a in range(5):
        moved = matrix[8 * a : 8 * a + 8]
        if a:
            moved = pltpu.roll(moved, OFFS[a] - 8 * a, axis=1)
        inside = (lane8 >= OFFS[a]) & (lane8 < OFFS[a] + 40 - 8 * a)
        out = jnp.where(inside, moved, out)
    for value, sub, first, start in (
        [(right, m, 8 * m, 120) for m in range(5)]
        + [(damp, 5 + m, 8 * m, 120) for m in range(3)]
        + [(damp, 6, 24, 112), (damp, 7, 32, 112)]
    ):
        moved = pltpu.roll(value, start - first, axis=1)
        inside = (sub8 == sub) & (lane8 >= start) & (lane8 < start + 8)
        out = jnp.where(inside, moved, out)
    tiles[HALF - 1] = out
    for g in (2, 1, 0):
        for i in GROUPS[g]:
            send(tiles.at[HALF - 1], tiles.at[i], 5, SAME[i], group_sem.at[g])
    for g in range(3):
        at, n = GROUPS[g][0], len(GROUPS[g])
        wait(tiles.at[pl.ds(at, n)], group_sem.at[g])
        n += g == 0
        send(tiles.at[pl.ds(at, n)], tiles.at[pl.ds(HALF + at, n)], 6, PAIR)
    wait(tiles.at[pl.ds(HALF, HALF)], recv_sem.at[6])

    for r in range(8):
        turned[r] = tiles[:, r, :].T
    rhs = jnp.concatenate([turned[m, 120:128] for m in range(5)], axis=0)
    damping = jnp.concatenate(
        [turned[5, 120:128], turned[6, 120:128], turned[7, 120:128], turned[6, 112:120],
         turned[7, 112:120]], axis=0,
    )
    id_lanes = damping[PARAMS : PARAMS + 1]
    row40 = lax.broadcasted_iota(jnp.int32, (40, N), 0)
    damping = jnp.where(row40 < PARAMS, damping, 0.0)
    id_subs = tiles[:, 7, 112 + 6 : 112 + 7]
    same = id_subs == id_lanes
    earlier = lax.broadcasted_iota(jnp.int32, (N, N), 0) < lax.broadcasted_iota(jnp.int32, (N, N), 1)
    repeats = jnp.sum(jnp.where(same & earlier, 1.0, 0.0), axis=0, keepdims=True)
    once = jnp.where(repeats == 0.0, 1.0, 0.0)
    same = same.astype(B)

    def total(v):
        return jnp.sum(jnp.sum(v * once, axis=0, keepdims=True), axis=1, keepdims=True)

    def operator(v):
        product = matvec(turned, [v[8 * a : 8 * a + 8] for a in range(5)])
        return dot_ones(jnp.concatenate(product, axis=0), same, ((1,), (0,))) + damping * v

    remainder = dot_ones(rhs, same, ((1,), (0,)))
    direction = remainder
    norm = total(remainder * remainder)
    answered = jnp.zeros_like(remainder)
    for it in range(CG_ITERS):
        image = operator(direction)
        step = norm / total(direction * image)
        answered = answered + step * direction
        remainder = remainder - step * image
        if it + 1 < CG_ITERS:
            norm_next = total(remainder * remainder)
            direction = remainder + (norm_next / norm) * direction
            norm = norm_next
    result_out[0:40] = answered * once
    result_out[40:80] = remainder * once
    result_out[80:88] = jnp.broadcast_to(id_lanes, (8, N))
    wait(ids.at[pl.ds(0, ASKERS - 1)], send_sem.at[0])
    wait(owned.at[pl.ds(1, 3)], send_sem.at[1])
    wait(owned_damping.at[pl.ds(1, 3)], send_sem.at[2])
    wait(columns.at[pl.ds(0, ASKERS - 1)], send_sem.at[3])
    wait(columns_damping.at[pl.ds(0, ASKERS - 1)], send_sem.at[4])
    wait(tiles.at[pl.ds(0, HALF - 1)], send_sem.at[5])
    wait(tiles.at[pl.ds(HALF, HALF)], send_sem.at[6])


def place(result, update_out, residual_out):
    first = ((lax.axis_index("cam") * 16 + lax.axis_index("ray")) * COLS).astype(F)
    count = lax.broadcasted_iota(jnp.int32, (COLS, N), 0).astype(F)
    where = (result[80:81] - first == count).astype(B)
    out = dot_ones(result[0:80], where, ((1,), (1,)))
    update_out[...] = out[0:PARAMS]
    residual_out[...] = out[40 : 40 + PARAMS]


def body(encodings, ray_camera, targets, weights, head_weight, quadrature, lift, cam_params, damping):
    vmem = pl.BlockSpec(memory_space=pltpu.VMEM)
    smem = pl.BlockSpec(memory_space=pltpu.SMEM)
    hbm = pl.BlockSpec(memory_space=pl.ANY)
    result = pl.pallas_call(
        kernel,
        out_shape=jax.ShapeDtypeStruct((88, N), F),
        in_specs=[smem] + [hbm] * 8,
        out_specs=vmem,
        scratch_shapes=[
            pltpu.VMEM((RAYS, SAMPLES, D), B),
            pltpu.VMEM((COLORS, RAYS), F),
            pltpu.VMEM((LAYERS, D, D), B),
            pltpu.VMEM((COLORS, D), B),
            pltpu.VMEM((PARAMS, D), F),
            pltpu.VMEM((LAYERS, D, D), B),
            pltpu.VMEM((D, D), F),
            pltpu.VMEM((SAMPLES, D), F),
            pltpu.VMEM((ASKERS, 1, RAYS), jnp.int32),
            pltpu.VMEM((4, PARAMS, COLS), F),
            pltpu.VMEM((4, PARAMS, COLS), F),
            pltpu.VMEM((ASKERS, 1, D), F),
            pltpu.VMEM((ASKERS, 1, D), F),
            pltpu.VMEM((ASKERS, 1, D), F),
            pltpu.VMEM((ASKERS, 1, D), F),
            pltpu.VMEM((COLORS, RAYS, D), F),
            pltpu.VMEM((RAYS, D), F),
            pltpu.VMEM((N, 8, D), F),
            pltpu.VMEM((8, D, N), F),
            pltpu.SemaphoreType.DMA((8,)),
            pltpu.SemaphoreType.DMA((7,)),
            pltpu.SemaphoreType.DMA((7,)),
            pltpu.SemaphoreType.DMA((3,)),
        ],
        name="pose_solve",
        compiler_params=pltpu.CompilerParams(
            collective_id=0, has_side_effects=True, vmem_limit_bytes=60 * 2**20
        ),
    )(
        quadrature, ray_camera.reshape(1, RAYS), encodings, targets.T, weights, head_weight.T, lift,
        cam_params, damping,
    )
    out = jax.ShapeDtypeStruct((PARAMS, COLS), F)
    return pl.pallas_call(
        place, out_shape=(out, out), in_specs=[vmem], out_specs=(vmem, vmem), name="pose_place"
    )(result)


def solution(mesh):
    in_specs = (
        P(BOTH, None, None), P(BOTH), P(BOTH, None), P(), P(), P(), P(), P(None, BOTH), P(None, BOTH),
    )
    out_specs = (P(None, BOTH), P(None, BOTH))
    return jax.shard_map(body, mesh=mesh, in_specs=in_specs, out_specs=out_specs, check_vma=False)
```

```python
import functools

import jax
import jax.numpy as jnp
from jax import lax
from jax.experimental import pallas as pl
from jax.experimental.pallas import tpu as pltpu
from jax.sharding import PartitionSpec as P

F = jnp.float32
B = jnp.bfloat16
MESH = pl.DeviceIdType.MESH
BOTH = ("cam", "ray")
N = 128
D = 128
SAMPLES = 48
COLORS = 3
RAYS = 64
LAYERS = 4
PARAMS = 38
COLS = 256
CG_ITERS = 2
STEP_RAYS = 64
HI = lax.Precision.HIGHEST
OFFS = (0, 40, 72, 96, 112)


def far(o):
    return sum(min(d, 4 - d) for d in (o[0], o[2], o[3]))


OTHERS = sorted(
    (
        (dz, dc, dy, dx)
        for dz in range(4)
        for dc in range(2)
        for dy in range(4)
        for dx in range(4)
        if (dz, dc, dy, dx) != (0, 0, 0, 0)
    ),
    key=lambda o: -far(o),
)
ROW = [(dc, dy) for dc, dy in ((0, 2), (1, 2), (0, 1), (0, 3), (1, 1), (1, 3), (1, 0), (0, 0))]
PLANE = [(dz, dc, dy, 0) for dz in range(4) for dc, dy in ROW]
OWN = len(ROW) - 1
ROWS = [(0, dc, dy, 0) for dc, dy in ROW[:OWN]]
COLUMN = [(dz, 0, 0, 0) for dz in (2, 1, 3)]
LINE = [(0, 0, 0, dx) for dx in (2, 1, 3)]
SAME = [o for o in OTHERS if o[1] == 0]
PAIR = (0, 1, 0, 0)
ANSWERED = sorted((i for i in range(len(PLANE)) if i != OWN), key=lambda i: -far(PLANE[i]))
ASKERS = len(PLANE)
HALF = len(SAME) + 1
GROUPS = [[i for i, o in enumerate(SAME) if far(o) in hops] for hops in ((1, 2), (3,), (4, 5, 6))]


def device(o):
    cam, ray = lax.axis_index("cam"), lax.axis_index("ray")
    z, c, y, x = cam // 2, cam % 2, ray // 4, ray % 4
    return (z + o[0]) % 4 * 2 + (c + o[1]) % 2, (y + o[2]) % 4 * 4 + (x + o[3]) % 4


def opposite(o):
    return (-o[0]) % 4, (-o[1]) % 2, (-o[2]) % 4, (-o[3]) % 4


def dot(a, b, dims, precision=HI):
    return lax.dot_general(a, b, (dims, ((), ())), precision=precision, preferred_element_type=F)


def three_terms(a):
    high = a.astype(B)
    rest = a - high.astype(F)
    middle = rest.astype(B)
    low = (rest - middle.astype(F)).astype(B)
    return jnp.concatenate([high, middle, low], axis=0)


def dot_terms(terms, b, dims):
    n = terms.shape[0] // 3
    out = dot(terms, b, dims, None)
    return out[0:n] + out[n : 2 * n] + out[2 * n : 3 * n]


def dot_ones(a, b, dims):
    return dot_terms(three_terms(a), b, dims)


def mlp(enc, de, w, wt, hw, quad, depth, grads, mixed):
    rows = STEP_RAYS * SAMPLES
    quad, depth = quad[None], depth[None]

    def step(t, carry):
        at = pl.ds(pl.multiple_of(t * STEP_RAYS, STEP_RAYS), STEP_RAYS)
        h = jnp.tanh(enc[at].astype(F) + de[None]).astype(B).reshape(rows, D)
        hs = [h]
        for layer in range(LAYERS):
            h = jnp.tanh(jnp.dot(h, w[layer], preferred_element_type=F)).astype(B)
            hs.append(h)
        last = h.astype(F).reshape(STEP_RAYS, SAMPLES, D)
        mixed[at] = jnp.sum(quad * last, axis=1)
        slope = ((1.0 - last * last) * quad).reshape(rows, D)
        ys = [(slope * hw[c : c + 1]).astype(B) for c in range(COLORS)]
        for layer in range(LAYERS - 1, 0, -1):
            inner = hs[layer].astype(F)
            slope = 1.0 - inner * inner
            ys = [(jnp.dot(y, wt[layer], preferred_element_type=F) * slope).astype(B) for y in ys]
        first = hs[0].astype(F).reshape(STEP_RAYS, SAMPLES, D)
        slope = (1.0 - first * first) * depth
        for c in range(COLORS):
            inner = jnp.dot(ys[c], wt[0], preferred_element_type=F)
            grads[c, at] = jnp.sum(inner.reshape(STEP_RAYS, SAMPLES, D) * slope, axis=1)
        return carry

    lax.fori_loop(0, RAYS // STEP_RAYS, step, 0)


def matvec(turned, v):
    sub = lax.broadcasted_iota(jnp.int32, (8, N), 0)
    outs = [jnp.zeros((8, N), F) for _ in range(5)]
    for r in range(8):
        for a in range(5):
            if 8 * a + r >= PARAMS:
                continue
            own = v[a][r : r + 1]
            total = None
            for j in range(a, 5):
                at = OFFS[a] + 8 * (j - a)
                piece = turned[r, at : at + 8]
                term = piece * v[j]
                total = term if total is None else total + term
                if j > a:
                    outs[j] = outs[j] + piece * own
            row = jnp.sum(total, axis=0, keepdims=True)
            outs[a] = outs[a] + jnp.where(sub == r, row, 0.0)
    return outs


def kernel(
    quad_in, ids_in, enc_in, targets_in, w_in, hw_in, lift_in, params_in, damping_in,
    result_out,
    enc, targets, w, hw_b, lift_b, quad_b, wt, lift, quad, ids, owned, owned_damping,
    reply, reply_damping, columns, columns_damping, grads, mixed, tiles, turned,
    load_sem, send_sem, recv_sem, group_sem,
):
    def send(source, target, n, o, recv=None):
        pltpu.make_async_remote_copy(
            source, target, send_sem.at[n], recv_sem.at[n] if recv is None else recv,
            device_id=device(o), device_id_type=MESH,
        ).start()

    def wait(ref, sem):
        pltpu.make_async_copy(ref, ref, sem).wait()

    barrier = pltpu.get_barrier_semaphore()
    for o in ROWS + COLUMN + LINE:
        pl.semaphore_signal(barrier, inc=1, device_id=device(o), device_id_type=MESH)
    loads = [
        pltpu.make_async_copy(source, target, load_sem.at[i])
        for i, (source, target) in enumerate(
            [
                (ids_in, ids.at[OWN]),
                (params_in, owned.at[0]),
                (damping_in, owned_damping.at[0]),
                (lift_in, lift_b),
                (w_in, w),
                (hw_in, hw_b),
                (targets_in, targets),
                (quad_in, quad_b),
                (enc_in, enc),
            ]
        )
    ]
    for load in loads:
        load.start()

    reply[...] = jnp.zeros_like(reply)
    reply_damping[...] = jnp.zeros_like(reply_damping)
    lift[...] = jnp.zeros_like(lift)
    depth = (lax.broadcasted_iota(jnp.int32, (SAMPLES, D), 0).astype(F) + 1.0) / SAMPLES
    loads[0].wait()
    loads[1].wait()
    pl.semaphore_wait(barrier, len(ROWS) + len(COLUMN) + len(LINE))

    for i, o in enumerate(ROWS):
        send(ids.at[OWN], ids.at[i], 0, o)
    for o in LINE:
        send(owned.at[0], owned.at[o[3]], 1, o)
    loads[2].wait()
    for o in LINE:
        send(owned_damping.at[0], owned_damping.at[o[3]], 2, o)
    for load in loads[3:8]:
        load.wait()
    lift[0:PARAMS] = lift_b[...]
    quad[...] = jnp.broadcast_to(quad_b[...], (D, SAMPLES)).T
    hw = hw_b[...].astype(F)
    wait(ids.at[pl.ds(0, OWN)], recv_sem.at[0])
    row = ids.at[pl.ds(0, OWN + 1)]
    for o in COLUMN:
        send(row, ids.at[pl.ds(o[0] * (OWN + 1), OWN + 1)], 7, o)
    for layer in range(LAYERS):
        wt[layer] = w[layer].T

    def terms_of(held):
        wide = jnp.concatenate([held[t] for t in range(4)], axis=1)
        return three_terms(jnp.concatenate([wide, jnp.zeros((2, 4 * COLS), F)], axis=0))

    wait(owned.at[pl.ds(1, 3)], recv_sem.at[1])
    terms = terms_of(owned)
    wait(ids.at[pl.ds(OWN + 1, 3 * (OWN + 1))], recv_sem.at[7])

    asked = ids[...].reshape(ASKERS, RAYS).astype(F)
    here = lax.broadcasted_iota(jnp.int32, (ASKERS, RAYS), 0) == lax.broadcasted_iota(
        jnp.int32, (ASKERS, RAYS), 1
    )
    asked = jnp.sum(jnp.where(here, asked, 0.0), axis=0, keepdims=True)
    count = lax.broadcasted_iota(jnp.int32, (COLS, RAYS), 0).astype(F)
    picked = []
    for t in range(4):
        cam, ray = device((0, 0, 0, (4 - t) % 4))
        first = ((cam * 16 + ray) * COLS).astype(F)
        picked.append((asked - first == count).astype(B))
    picked = jnp.concatenate(picked, axis=0)

    def answer(terms, rows, landing, n):
        got = dot_terms(terms, picked, ((1,), (0,)))
        rows[:, 0, 0:40] = got.T[0:ASKERS]
        for i in ANSWERED:
            send(rows.at[i], landing.at[i], n, opposite(PLANE[i]))
        landing[OWN] = rows[OWN]

    answer(terms, reply, columns, 3)
    wait(owned_damping.at[pl.ds(1, 3)], recv_sem.at[2])
    answer(terms_of(owned_damping), reply_damping, columns_damping, 4)
    wait(columns.at[pl.ds(0, ASKERS - 1)], recv_sem.at[3])
    column = jnp.sum(columns[...].reshape(ASKERS, D), axis=0, keepdims=True)
    lifted = dot(jnp.broadcast_to(column, (8, D)), lift[...], ((1,), (0,)))[0:1]
    loads[8].wait()
    mlp(enc, depth * lifted, w, wt, hw, quad[...], depth, grads, mixed)

    wait(columns_damping.at[pl.ds(0, ASKERS - 1)], recv_sem.at[4])
    damp = jnp.sum(columns_damping[...].reshape(ASKERS, D), axis=0, keepdims=True)
    residual = dot(hw, mixed[...], ((1,), (1,))) - targets[...]
    lane8 = lax.broadcasted_iota(jnp.int32, (8, D), 1)
    sub8 = lax.broadcasted_iota(jnp.int32, (8, D), 0)
    rows = dot(grads[...].reshape(COLORS * RAYS, D), lift[...], ((1,), (1,)))
    matrix = dot(rows.T[0:40], rows, ((1,), (0,)))
    right = jnp.zeros((1, D), F)
    for c in range(COLORS):
        part = rows[c * RAYS : (c + 1) * RAYS]
        right = right - dot(residual[c : c + 1], part, ((1,), (0,)))
    right = jnp.broadcast_to(right, (8, D))
    camera = ids[OWN][:, 0:1].astype(F)
    damp = jnp.where(lane8 == PARAMS, camera, jnp.broadcast_to(damp, (8, D)))
    out = jnp.zeros((8, D), F)
    for a in range(5):
        moved = matrix[8 * a : 8 * a + 8]
        if a:
            moved = pltpu.roll(moved, OFFS[a] - 8 * a, axis=1)
        inside = (lane8 >= OFFS[a]) & (lane8 < OFFS[a] + 40 - 8 * a)
        out = jnp.where(inside, moved, out)
    for value, sub, first, start in (
        [(right, m, 8 * m, 120) for m in range(5)]
        + [(damp, 5 + m, 8 * m, 120) for m in range(3)]
        + [(damp, 6, 24, 112), (damp, 7, 32, 112)]
    ):
        moved = pltpu.roll(value, start - first, axis=1)
        inside = (sub8 == sub) & (lane8 >= start) & (lane8 < start + 8)
        out = jnp.where(inside, moved, out)
    tiles[HALF - 1] = out
    for g in (2, 1, 0):
        for i in GROUPS[g]:
            send(tiles.at[HALF - 1], tiles.at[i], 5, SAME[i], group_sem.at[g])
    for g in range(3):
        at, n = GROUPS[g][0], len(GROUPS[g])
        wait(tiles.at[pl.ds(at, n)], group_sem.at[g])
        n += g == 0
        send(tiles.at[pl.ds(at, n)], tiles.at[pl.ds(HALF + at, n)], 6, PAIR)
    wait(tiles.at[pl.ds(HALF, HALF)], recv_sem.at[6])

    for r in range(8):
        turned[r] = tiles[:, r, :].T
    rhs = jnp.concatenate([turned[m, 120:128] for m in range(5)], axis=0)
    damping = jnp.concatenate(
        [turned[5, 120:128], turned[6, 120:128], turned[7, 120:128], turned[6, 112:120],
         turned[7, 112:120]], axis=0,
    )
    id_lanes = damping[PARAMS : PARAMS + 1]
    row40 = lax.broadcasted_iota(jnp.int32, (40, N), 0)
    damping = jnp.where(row40 < PARAMS, damping, 0.0)
    id_subs = tiles[:, 7, 112 + 6 : 112 + 7]
    same = id_subs == id_lanes
    earlier = lax.broadcasted_iota(jnp.int32, (N, N), 0) < lax.broadcasted_iota(jnp.int32, (N, N), 1)
    repeats = jnp.sum(jnp.where(same & earlier, 1.0, 0.0), axis=0, keepdims=True)
    once = jnp.where(repeats == 0.0, 1.0, 0.0)
    same = same.astype(B)

    def total(v):
        return jnp.sum(jnp.sum(v * once, axis=0, keepdims=True), axis=1, keepdims=True)

    def operator(v):
        product = matvec(turned, [v[8 * a : 8 * a + 8] for a in range(5)])
        return dot_ones(jnp.concatenate(product, axis=0), same, ((1,), (0,))) + damping * v

    remainder = dot_ones(rhs, same, ((1,), (0,)))
    direction = remainder
    norm = total(remainder * remainder)
    answered = jnp.zeros_like(remainder)
    for it in range(CG_ITERS):
        image = operator(direction)
        step = norm / total(direction * image)
        answered = answered + step * direction
        remainder = remainder - step * image
        if it + 1 < CG_ITERS:
            norm_next = total(remainder * remainder)
            direction = remainder + (norm_next / norm) * direction
            norm = norm_next
    result_out[0:40] = answered * once
    result_out[40:80] = remainder * once
    result_out[80:88] = jnp.broadcast_to(id_lanes, (8, N))
    wait(ids.at[pl.ds(0, OWN)], send_sem.at[0])
    wait(ids.at[pl.ds(OWN + 1, 3 * (OWN + 1))], send_sem.at[7])
    wait(owned.at[pl.ds(1, 3)], send_sem.at[1])
    wait(owned_damping.at[pl.ds(1, 3)], send_sem.at[2])
    wait(columns.at[pl.ds(0, ASKERS - 1)], send_sem.at[3])
    wait(columns_damping.at[pl.ds(0, ASKERS - 1)], send_sem.at[4])
    wait(tiles.at[pl.ds(0, HALF - 1)], send_sem.at[5])
    wait(tiles.at[pl.ds(HALF, HALF)], send_sem.at[6])


def place(result, update_out, residual_out):
    first = ((lax.axis_index("cam") * 16 + lax.axis_index("ray")) * COLS).astype(F)
    count = lax.broadcasted_iota(jnp.int32, (COLS, N), 0).astype(F)
    where = (result[80:81] - first == count).astype(B)
    out = dot_ones(result[0:80], where, ((1,), (1,)))
    update_out[...] = out[0:PARAMS]
    residual_out[...] = out[40 : 40 + PARAMS]


def body(encodings, ray_camera, targets, weights, head_weight, quadrature, lift, cam_params, damping):
    vmem = pl.BlockSpec(memory_space=pltpu.VMEM)
    hbm = pl.BlockSpec(memory_space=pl.ANY)
    result = pl.pallas_call(
        kernel,
        out_shape=jax.ShapeDtypeStruct((88, N), F),
        in_specs=[hbm] * 9,
        out_specs=vmem,
        scratch_shapes=[
            pltpu.VMEM((RAYS, SAMPLES, D), B),
            pltpu.VMEM((COLORS, RAYS), F),
            pltpu.VMEM((LAYERS, D, D), B),
            pltpu.VMEM((COLORS, D), B),
            pltpu.VMEM((PARAMS, D), F),
            pltpu.VMEM((1, SAMPLES), F),
            pltpu.VMEM((LAYERS, D, D), B),
            pltpu.VMEM((D, D), F),
            pltpu.VMEM((SAMPLES, D), F),
            pltpu.VMEM((ASKERS, 1, RAYS), jnp.int32),
            pltpu.VMEM((4, PARAMS, COLS), F),
            pltpu.VMEM((4, PARAMS, COLS), F),
            pltpu.VMEM((ASKERS, 1, D), F),
            pltpu.VMEM((ASKERS, 1, D), F),
            pltpu.VMEM((ASKERS, 1, D), F),
            pltpu.VMEM((ASKERS, 1, D), F),
            pltpu.VMEM((COLORS, RAYS, D), F),
            pltpu.VMEM((RAYS, D), F),
            pltpu.VMEM((N, 8, D), F),
            pltpu.VMEM((8, D, N), F),
            pltpu.SemaphoreType.DMA((9,)),
            pltpu.SemaphoreType.DMA((8,)),
            pltpu.SemaphoreType.DMA((8,)),
            pltpu.SemaphoreType.DMA((3,)),
        ],
        name="pose_solve",
        compiler_params=pltpu.CompilerParams(
            collective_id=0, has_side_effects=True, vmem_limit_bytes=60 * 2**20
        ),
    )(
        quadrature.reshape(1, SAMPLES), ray_camera.reshape(1, RAYS), encodings, targets.T, weights, head_weight.T, lift,
        cam_params, damping,
    )
    out = jax.ShapeDtypeStruct((PARAMS, COLS), F)
    return pl.pallas_call(
        place, out_shape=(out, out), in_specs=[vmem], out_specs=(vmem, vmem), name="pose_place"
    )(result)


def solution(mesh):
    in_specs = (
        P(BOTH, None, None), P(BOTH), P(BOTH, None), P(), P(), P(), P(), P(None, BOTH), P(None, BOTH),
    )
    out_specs = (P(None, BOTH), P(None, BOTH))
    return jax.shard_map(body, mesh=mesh, in_specs=in_specs, out_specs=out_specs, check_vma=False)
```

```python
import functools

import jax
import jax.numpy as jnp
from jax import lax
from jax.experimental import pallas as pl
from jax.experimental.pallas import tpu as pltpu
from jax.sharding import PartitionSpec as P

F = jnp.float32
B = jnp.bfloat16
MESH = pl.DeviceIdType.MESH
BOTH = ("cam", "ray")
N = 128
D = 128
SAMPLES = 48
COLORS = 3
RAYS = 64
LAYERS = 4
PARAMS = 38
COLS = 256
CG_ITERS = 2
STEP_RAYS = 64
HI = lax.Precision.HIGHEST
OFFS = (0, 40, 72, 96, 112)


def far(o):
    return sum(min(d, 4 - d) for d in (o[0], o[2], o[3]))


OTHERS = sorted(
    (
        (dz, dc, dy, dx)
        for dz in range(4)
        for dc in range(2)
        for dy in range(4)
        for dx in range(4)
        if (dz, dc, dy, dx) != (0, 0, 0, 0)
    ),
    key=lambda o: -far(o),
)
ROW = [(dc, dy) for dc, dy in ((0, 2), (1, 2), (0, 1), (0, 3), (1, 1), (1, 3), (1, 0), (0, 0))]
PLANE = [(dz, dc, dy, 0) for dz in range(4) for dc, dy in ROW]
OWN = len(ROW) - 1
ROWS = [(0, dc, dy, 0) for dc, dy in ROW[:OWN]]
COLUMN = [(dz, 0, 0, 0) for dz in (2, 1, 3)]
LINE = [(0, 0, 0, dx) for dx in (2, 1, 3)]
SAME = [o for o in OTHERS if o[1] == 0]
PAIR = (0, 1, 0, 0)
ANSWERED = sorted((i for i in range(len(PLANE)) if i != OWN), key=lambda i: -far(PLANE[i]))
ASKERS = len(PLANE)
HALF = len(SAME) + 1
GROUPS = [[i for i, o in enumerate(SAME) if far(o) in hops] for hops in ((1, 2), (3,), (4, 5, 6))]


def device(o):
    cam, ray = lax.axis_index("cam"), lax.axis_index("ray")
    z, c, y, x = cam // 2, cam % 2, ray // 4, ray % 4
    return (z + o[0]) % 4 * 2 + (c + o[1]) % 2, (y + o[2]) % 4 * 4 + (x + o[3]) % 4


def opposite(o):
    return (-o[0]) % 4, (-o[1]) % 2, (-o[2]) % 4, (-o[3]) % 4


def dot(a, b, dims, precision=HI):
    return lax.dot_general(a, b, (dims, ((), ())), precision=precision, preferred_element_type=F)


def three_terms(a):
    high = a.astype(B)
    rest = a - high.astype(F)
    middle = rest.astype(B)
    low = (rest - middle.astype(F)).astype(B)
    return jnp.concatenate([high, middle, low], axis=0)


def two_terms(a, axis):
    high = a.astype(B)
    return jnp.concatenate([high, (a - high.astype(F)).astype(B)], axis=axis)


def dot_two(a, b, dims):
    out = dot(a, b, dims, None)
    m, n = out.shape[0] // 2, out.shape[1] // 2
    return (out[0:m, 0:n] + (out[0:m, n:] + out[m:, 0:n])) + out[m:, n:]


def dot_terms(terms, b, dims):
    n = terms.shape[0] // 3
    out = dot(terms, b, dims, None)
    return out[0:n] + out[n : 2 * n] + out[2 * n : 3 * n]


def dot_ones(a, b, dims):
    return dot_terms(three_terms(a), b, dims)


def mlp(enc, de, w, wt, hw, quad, depth, grads, mixed):
    rows = STEP_RAYS * SAMPLES
    quad, depth = quad[None], depth[None]

    def step(t, carry):
        at = pl.ds(pl.multiple_of(t * STEP_RAYS, STEP_RAYS), STEP_RAYS)
        h = jnp.tanh(enc[at].astype(F) + de[None]).astype(B).reshape(rows, D)
        hs = [h]
        for layer in range(LAYERS):
            h = jnp.tanh(jnp.dot(h, w[layer], preferred_element_type=F)).astype(B)
            hs.append(h)
        last = h.astype(F).reshape(STEP_RAYS, SAMPLES, D)
        mixed[at] = jnp.sum(quad * last, axis=1)
        slope = ((1.0 - last * last) * quad).reshape(rows, D)
        ys = [(slope * hw[c : c + 1]).astype(B) for c in range(COLORS)]
        for layer in range(LAYERS - 1, 0, -1):
            inner = hs[layer].astype(F)
            slope = 1.0 - inner * inner
            ys = [(jnp.dot(y, wt[layer], preferred_element_type=F) * slope).astype(B) for y in ys]
        first = hs[0].astype(F).reshape(STEP_RAYS, SAMPLES, D)
        slope = (1.0 - first * first) * depth
        for c in range(COLORS):
            inner = jnp.dot(ys[c], wt[0], preferred_element_type=F)
            grads[c, at] = jnp.sum(inner.reshape(STEP_RAYS, SAMPLES, D) * slope, axis=1)
        return carry

    lax.fori_loop(0, RAYS // STEP_RAYS, step, 0)


def matvec(turned, v):
    sub = lax.broadcasted_iota(jnp.int32, (8, N), 0)
    outs = [jnp.zeros((8, N), F) for _ in range(5)]
    for r in range(8):
        for a in range(5):
            if 8 * a + r >= PARAMS:
                continue
            own = v[a][r : r + 1]
            total = None
            for j in range(a, 5):
                at = OFFS[a] + 8 * (j - a)
                piece = turned[r, at : at + 8]
                term = piece * v[j]
                total = term if total is None else total + term
                if j > a:
                    outs[j] = outs[j] + piece * own
            row = jnp.sum(total, axis=0, keepdims=True)
            outs[a] = outs[a] + jnp.where(sub == r, row, 0.0)
    return outs


def kernel(
    quad_in, ids_in, enc_in, targets_in, w_in, hw_in, lift_in, params_in, damping_in,
    result_out,
    enc, targets, w, hw_b, lift_b, quad_b, wt, lift, lift2, quad, ids, owned, owned_damping,
    reply, reply_damping, columns, columns_damping, grads, mixed, tiles, turned,
    load_sem, send_sem, recv_sem, group_sem,
):
    def send(source, target, n, o, recv=None):
        pltpu.make_async_remote_copy(
            source, target, send_sem.at[n], recv_sem.at[n] if recv is None else recv,
            device_id=device(o), device_id_type=MESH,
        ).start()

    def wait(ref, sem):
        pltpu.make_async_copy(ref, ref, sem).wait()

    barrier = pltpu.get_barrier_semaphore()
    for o in ROWS + COLUMN + LINE:
        pl.semaphore_signal(barrier, inc=1, device_id=device(o), device_id_type=MESH)
    loads = [
        pltpu.make_async_copy(source, target, load_sem.at[i])
        for i, (source, target) in enumerate(
            [
                (ids_in, ids.at[OWN]),
                (params_in, owned.at[0]),
                (damping_in, owned_damping.at[0]),
                (lift_in, lift_b),
                (w_in, w),
                (hw_in, hw_b),
                (targets_in, targets),
                (quad_in, quad_b),
                (enc_in, enc),
            ]
        )
    ]
    for load in loads:
        load.start()

    reply[...] = jnp.zeros_like(reply)
    reply_damping[...] = jnp.zeros_like(reply_damping)
    lift[...] = jnp.zeros_like(lift)
    depth = (lax.broadcasted_iota(jnp.int32, (SAMPLES, D), 0).astype(F) + 1.0) / SAMPLES
    loads[0].wait()
    loads[1].wait()
    pl.semaphore_wait(barrier, len(ROWS) + len(COLUMN) + len(LINE))

    for i, o in enumerate(ROWS):
        send(ids.at[OWN], ids.at[i], 0, o)
    for o in LINE:
        send(owned.at[0], owned.at[o[3]], 1, o)
    loads[2].wait()
    for o in LINE:
        send(owned_damping.at[0], owned_damping.at[o[3]], 2, o)
    for load in loads[3:8]:
        load.wait()
    lift[0:PARAMS] = lift_b[...]
    lift2[...] = two_terms(lift[...], 0)
    quad[...] = jnp.broadcast_to(quad_b[...], (D, SAMPLES)).T
    hw = hw_b[...].astype(F)
    wait(ids.at[pl.ds(0, OWN)], recv_sem.at[0])
    row = ids.at[pl.ds(0, OWN + 1)]
    for o in COLUMN:
        send(row, ids.at[pl.ds(o[0] * (OWN + 1), OWN + 1)], 7, o)
    for layer in range(LAYERS):
        wt[layer] = w[layer].T

    def terms_of(held):
        wide = jnp.concatenate([held[t] for t in range(4)], axis=1)
        return three_terms(jnp.concatenate([wide, jnp.zeros((2, 4 * COLS), F)], axis=0))

    wait(owned.at[pl.ds(1, 3)], recv_sem.at[1])
    terms = terms_of(owned)
    wait(ids.at[pl.ds(OWN + 1, 3 * (OWN + 1))], recv_sem.at[7])

    asked = ids[...].reshape(ASKERS, RAYS).astype(F)
    here = lax.broadcasted_iota(jnp.int32, (ASKERS, RAYS), 0) == lax.broadcasted_iota(
        jnp.int32, (ASKERS, RAYS), 1
    )
    asked = jnp.sum(jnp.where(here, asked, 0.0), axis=0, keepdims=True)
    count = lax.broadcasted_iota(jnp.int32, (COLS, RAYS), 0).astype(F)
    picked = []
    for t in range(4):
        cam, ray = device((0, 0, 0, (4 - t) % 4))
        first = ((cam * 16 + ray) * COLS).astype(F)
        picked.append((asked - first == count).astype(B))
    picked = jnp.concatenate(picked, axis=0)

    def answer(terms, rows, landing, n):
        got = dot_terms(terms, picked, ((1,), (0,)))
        rows[:, 0, 0:40] = got.T[0:ASKERS]
        for i in ANSWERED:
            send(rows.at[i], landing.at[i], n, opposite(PLANE[i]))
        landing[OWN] = rows[OWN]

    answer(terms, reply, columns, 3)
    wait(owned_damping.at[pl.ds(1, 3)], recv_sem.at[2])
    answer(terms_of(owned_damping), reply_damping, columns_damping, 4)
    wait(columns.at[pl.ds(0, ASKERS - 1)], recv_sem.at[3])
    column = jnp.sum(columns[...].reshape(ASKERS, D), axis=0, keepdims=True)
    lifted = dot(jnp.broadcast_to(column, (8, D)), lift[...], ((1,), (0,)))[0:1]
    loads[8].wait()
    mlp(enc, depth * lifted, w, wt, hw, quad[...], depth, grads, mixed)

    wait(columns_damping.at[pl.ds(0, ASKERS - 1)], recv_sem.at[4])
    damp = jnp.sum(columns_damping[...].reshape(ASKERS, D), axis=0, keepdims=True)
    residual = dot(hw, mixed[...], ((1,), (1,))) - targets[...]
    lane8 = lax.broadcasted_iota(jnp.int32, (8, D), 1)
    sub8 = lax.broadcasted_iota(jnp.int32, (8, D), 0)
    rows = dot_two(two_terms(grads[...].reshape(COLORS * RAYS, D), 0), lift2[...], ((1,), (1,)))
    residual = jnp.concatenate([residual[c : c + 1] for c in range(COLORS)], axis=1)
    left = jnp.concatenate([rows.T[0:40], jnp.broadcast_to(-residual, (8, COLORS * RAYS))], axis=0)
    matrix = dot_two(two_terms(left, 0), two_terms(rows, 1), ((1,), (0,)))
    right = matrix[40:48]
    camera = ids[OWN][:, 0:1].astype(F)
    damp = jnp.where(lane8 == PARAMS, camera, jnp.broadcast_to(damp, (8, D)))
    out = jnp.zeros((8, D), F)
    for a in range(5):
        moved = matrix[8 * a : 8 * a + 8]
        if a:
            moved = pltpu.roll(moved, OFFS[a] - 8 * a, axis=1)
        inside = (lane8 >= OFFS[a]) & (lane8 < OFFS[a] + 40 - 8 * a)
        out = jnp.where(inside, moved, out)
    for value, sub, first, start in (
        [(right, m, 8 * m, 120) for m in range(5)]
        + [(damp, 5 + m, 8 * m, 120) for m in range(3)]
        + [(damp, 6, 24, 112), (damp, 7, 32, 112)]
    ):
        moved = pltpu.roll(value, start - first, axis=1)
        inside = (sub8 == sub) & (lane8 >= start) & (lane8 < start + 8)
        out = jnp.where(inside, moved, out)
    tiles[HALF - 1] = out
    for g in (2, 1, 0):
        for i in GROUPS[g]:
            send(tiles.at[HALF - 1], tiles.at[i], 5, SAME[i], group_sem.at[g])
    for g in range(3):
        at, n = GROUPS[g][0], len(GROUPS[g])
        wait(tiles.at[pl.ds(at, n)], group_sem.at[g])
        n += g == 0
        send(tiles.at[pl.ds(at, n)], tiles.at[pl.ds(HALF + at, n)], 6, PAIR)
    wait(tiles.at[pl.ds(HALF, HALF)], recv_sem.at[6])

    for r in range(8):
        turned[r] = tiles[:, r, :].T
    rhs = jnp.concatenate([turned[m, 120:128] for m in range(5)], axis=0)
    damping = jnp.concatenate(
        [turned[5, 120:128], turned[6, 120:128], turned[7, 120:128], turned[6, 112:120],
         turned[7, 112:120]], axis=0,
    )
    id_lanes = damping[PARAMS : PARAMS + 1]
    row40 = lax.broadcasted_iota(jnp.int32, (40, N), 0)
    damping = jnp.where(row40 < PARAMS, damping, 0.0)
    id_subs = tiles[:, 7, 112 + 6 : 112 + 7]
    same = id_subs == id_lanes
    earlier = lax.broadcasted_iota(jnp.int32, (N, N), 0) < lax.broadcasted_iota(jnp.int32, (N, N), 1)
    repeats = jnp.sum(jnp.where(same & earlier, 1.0, 0.0), axis=0, keepdims=True)
    once = jnp.where(repeats == 0.0, 1.0, 0.0)
    same = same.astype(B)

    def total(v):
        return jnp.sum(jnp.sum(v * once, axis=0, keepdims=True), axis=1, keepdims=True)

    def operator(v):
        product = matvec(turned, [v[8 * a : 8 * a + 8] for a in range(5)])
        return dot_ones(jnp.concatenate(product, axis=0), same, ((1,), (0,))) + damping * v

    remainder = dot_ones(rhs, same, ((1,), (0,)))
    direction = remainder
    norm = total(remainder * remainder)
    answered = jnp.zeros_like(remainder)
    for it in range(CG_ITERS):
        image = operator(direction)
        step = norm / total(direction * image)
        answered = answered + step * direction
        remainder = remainder - step * image
        if it + 1 < CG_ITERS:
            norm_next = total(remainder * remainder)
            direction = remainder + (norm_next / norm) * direction
            norm = norm_next
    result_out[0:40] = answered * once
    result_out[40:80] = remainder * once
    result_out[80:88] = jnp.broadcast_to(id_lanes, (8, N))
    wait(ids.at[pl.ds(0, OWN)], send_sem.at[0])
    wait(ids.at[pl.ds(OWN + 1, 3 * (OWN + 1))], send_sem.at[7])
    wait(owned.at[pl.ds(1, 3)], send_sem.at[1])
    wait(owned_damping.at[pl.ds(1, 3)], send_sem.at[2])
    wait(columns.at[pl.ds(0, ASKERS - 1)], send_sem.at[3])
    wait(columns_damping.at[pl.ds(0, ASKERS - 1)], send_sem.at[4])
    wait(tiles.at[pl.ds(0, HALF - 1)], send_sem.at[5])
    wait(tiles.at[pl.ds(HALF, HALF)], send_sem.at[6])


def place(result, update_out, residual_out):
    first = ((lax.axis_index("cam") * 16 + lax.axis_index("ray")) * COLS).astype(F)
    count = lax.broadcasted_iota(jnp.int32, (COLS, N), 0).astype(F)
    where = (result[80:81] - first == count).astype(B)
    out = dot_ones(result[0:80], where, ((1,), (1,)))
    update_out[...] = out[0:PARAMS]
    residual_out[...] = out[40 : 40 + PARAMS]


def body(encodings, ray_camera, targets, weights, head_weight, quadrature, lift, cam_params, damping):
    vmem = pl.BlockSpec(memory_space=pltpu.VMEM)
    hbm = pl.BlockSpec(memory_space=pl.ANY)
    inputs = (
        quadrature.reshape(1, SAMPLES), ray_camera.reshape(1, RAYS), encodings, targets.T, weights,
        head_weight.T, lift, cam_params, damping,
    )
    result = pl.pallas_call(
        kernel,
        out_shape=jax.ShapeDtypeStruct((88, N), F),
        in_specs=[hbm] * 9,
        out_specs=vmem,
        scratch_shapes=[
            pltpu.VMEM((RAYS, SAMPLES, D), B),
            pltpu.VMEM((COLORS, RAYS), F),
            pltpu.VMEM((LAYERS, D, D), B),
            pltpu.VMEM((COLORS, D), B),
            pltpu.VMEM((PARAMS, D), F),
            pltpu.VMEM((1, SAMPLES), F),
            pltpu.VMEM((LAYERS, D, D), B),
            pltpu.VMEM((D, D), F),
            pltpu.VMEM((2 * D, D), B),
            pltpu.VMEM((SAMPLES, D), F),
            pltpu.VMEM((ASKERS, 1, RAYS), jnp.int32),
            pltpu.VMEM((4, PARAMS, COLS), F),
            pltpu.VMEM((4, PARAMS, COLS), F),
            pltpu.VMEM((ASKERS, 1, D), F),
            pltpu.VMEM((ASKERS, 1, D), F),
            pltpu.VMEM((ASKERS, 1, D), F),
            pltpu.VMEM((ASKERS, 1, D), F),
            pltpu.VMEM((COLORS, RAYS, D), F),
            pltpu.VMEM((RAYS, D), F),
            pltpu.VMEM((N, 8, D), F),
            pltpu.VMEM((8, D, N), F),
            pltpu.SemaphoreType.DMA((9,)),
            pltpu.SemaphoreType.DMA((8,)),
            pltpu.SemaphoreType.DMA((8,)),
            pltpu.SemaphoreType.DMA((3,)),
        ],
        name="pose_solve",
        compiler_params=pltpu.CompilerParams(
            collective_id=0, has_side_effects=True, vmem_limit_bytes=48 * 2**20
        ),
    )(
        *(pltpu.with_memory_space_constraint(x, pltpu.HBM) for x in inputs)
    )
    out = jax.ShapeDtypeStruct((PARAMS, COLS), F)
    return pl.pallas_call(
        place, out_shape=(out, out), in_specs=[vmem], out_specs=(vmem, vmem), name="pose_place",
        compiler_params=pltpu.CompilerParams(vmem_limit_bytes=8 * 2**20),
    )(result)


def solution(mesh):
    in_specs = (
        P(BOTH, None, None), P(BOTH), P(BOTH, None), P(), P(), P(), P(), P(None, BOTH), P(None, BOTH),
    )
    out_specs = (P(None, BOTH), P(None, BOTH))
    return jax.shard_map(body, mesh=mesh, in_specs=in_specs, out_specs=out_specs, check_vma=False)
```

```python
import functools

import jax
import jax.numpy as jnp
from jax import lax
from jax.experimental import pallas as pl
from jax.experimental.pallas import tpu as pltpu
from jax.sharding import PartitionSpec as P

F = jnp.float32
B = jnp.bfloat16
MESH = pl.DeviceIdType.MESH
BOTH = ("cam", "ray")
N = 128
D = 128
SAMPLES = 48
COLORS = 3
RAYS = 64
LAYERS = 4
PARAMS = 38
COLS = 256
CG_ITERS = 2
STEP_RAYS = 64
HI = lax.Precision.HIGHEST
OFFS = (0, 40, 72, 96, 112)


def far(o):
    return sum(min(d, 4 - d) for d in (o[0], o[2], o[3]))


OTHERS = sorted(
    (
        (dz, dc, dy, dx)
        for dz in range(4)
        for dc in range(2)
        for dy in range(4)
        for dx in range(4)
        if (dz, dc, dy, dx) != (0, 0, 0, 0)
    ),
    key=lambda o: -far(o),
)
ROW = [(dc, dy) for dc, dy in ((0, 2), (1, 2), (0, 1), (0, 3), (1, 1), (1, 3), (1, 0), (0, 0))]
PLANE = [(dz, dc, dy, 0) for dz in range(4) for dc, dy in ROW]
OWN = len(ROW) - 1
ROWS = [(0, dc, dy, 0) for dc, dy in ROW[:OWN]]
COLUMN = [(dz, 0, 0, 0) for dz in (2, 1, 3)]
LINE = [(0, 0, 0, dx) for dx in (2, 1, 3)]
SAME = [o for o in OTHERS if o[1] == 0]
PAIR = (0, 1, 0, 0)
ANSWERED = sorted((i for i in range(len(PLANE)) if i != OWN), key=lambda i: -far(PLANE[i]))
ASKERS = len(PLANE)
HALF = len(SAME) + 1
GROUPS = [[i for i, o in enumerate(SAME) if far(o) in hops] for hops in ((1, 2), (3,), (4, 5, 6))]


def device(o):
    cam, ray = lax.axis_index("cam"), lax.axis_index("ray")
    z, c, y, x = cam // 2, cam % 2, ray // 4, ray % 4
    return (z + o[0]) % 4 * 2 + (c + o[1]) % 2, (y + o[2]) % 4 * 4 + (x + o[3]) % 4


def opposite(o):
    return (-o[0]) % 4, (-o[1]) % 2, (-o[2]) % 4, (-o[3]) % 4


def dot(a, b, dims, precision=HI):
    return lax.dot_general(a, b, (dims, ((), ())), precision=precision, preferred_element_type=F)


def three_terms(a):
    high = a.astype(B)
    rest = a - high.astype(F)
    middle = rest.astype(B)
    low = (rest - middle.astype(F)).astype(B)
    return jnp.concatenate([high, middle, low], axis=0)


def two_terms(a, axis):
    high = a.astype(B)
    return jnp.concatenate([high, (a - high.astype(F)).astype(B)], axis=axis)


def dot_two(a, b, dims):
    out = dot(a, b, dims, None)
    m, n = out.shape[0] // 2, out.shape[1] // 2
    return (out[0:m, 0:n] + (out[0:m, n:] + out[m:, 0:n])) + out[m:, n:]


def dot_terms(terms, b, dims):
    n = terms.shape[0] // 3
    out = dot(terms, b, dims, None)
    return out[0:n] + out[n : 2 * n] + out[2 * n : 3 * n]


def dot_ones(a, b, dims):
    return dot_terms(three_terms(a), b, dims)


def mlp(enc, de, w, wt, hw, quad, depth, grads, mixed):
    rows = STEP_RAYS * SAMPLES
    quad, depth = quad[None], depth[None]

    def step(t, carry):
        at = pl.ds(pl.multiple_of(t * STEP_RAYS, STEP_RAYS), STEP_RAYS)
        h = jnp.tanh(enc[at].astype(F) + de[None]).astype(B).reshape(rows, D)
        hs = [h]
        for layer in range(LAYERS):
            h = jnp.tanh(jnp.dot(h, w[layer], preferred_element_type=F)).astype(B)
            hs.append(h)
        last = h.astype(F).reshape(STEP_RAYS, SAMPLES, D)
        mixed[at] = jnp.sum(quad * last, axis=1)
        slope = ((1.0 - last * last) * quad).reshape(rows, D)
        ys = [(slope * hw[c : c + 1]).astype(B) for c in range(COLORS)]
        for layer in range(LAYERS - 1, 0, -1):
            inner = hs[layer].astype(F)
            slope = 1.0 - inner * inner
            ys = [(jnp.dot(y, wt[layer], preferred_element_type=F) * slope).astype(B) for y in ys]
        first = hs[0].astype(F).reshape(STEP_RAYS, SAMPLES, D)
        slope = (1.0 - first * first) * depth
        for c in range(COLORS):
            inner = jnp.dot(ys[c], wt[0], preferred_element_type=F)
            grads[c, at] = jnp.sum(inner.reshape(STEP_RAYS, SAMPLES, D) * slope, axis=1)
        return carry

    lax.fori_loop(0, RAYS // STEP_RAYS, step, 0)


def matvec(turned, v):
    sub = lax.broadcasted_iota(jnp.int32, (8, N), 0)
    outs = [jnp.zeros((8, N), F) for _ in range(5)]
    for r in range(8):
        for a in range(5):
            if 8 * a + r >= PARAMS:
                continue
            own = v[a][r : r + 1]
            total = None
            for j in range(a, 5):
                at = OFFS[a] + 8 * (j - a)
                piece = turned[r, at : at + 8]
                term = piece * v[j]
                total = term if total is None else total + term
                if j > a:
                    outs[j] = outs[j] + piece * own
            row = jnp.sum(total, axis=0, keepdims=True)
            outs[a] = outs[a] + jnp.where(sub == r, row, 0.0)
    return outs


def kernel(
    quad_in, ids_in, enc_in, targets_in, w_in, hw_in, lift_in, params_in, damping_in,
    result_out,
    enc, targets, w, hw_b, lift_b, quad_b, wt, lift, lift2, quad, ids, owned, owned_damping,
    reply, reply_damping, columns, columns_damping, grads, mixed, tiles, turned,
    load_sem, send_sem, recv_sem, group_sem,
):
    def send(source, target, n, o, recv=None):
        pltpu.make_async_remote_copy(
            source, target, send_sem.at[n], recv_sem.at[n] if recv is None else recv,
            device_id=device(o), device_id_type=MESH,
        ).start()

    def wait(ref, sem):
        pltpu.make_async_copy(ref, ref, sem).wait()

    barrier = pltpu.get_barrier_semaphore()
    for o in [opposite(PLANE[i]) for i in ANSWERED] + LINE:
        pl.semaphore_signal(barrier, inc=1, device_id=device(o), device_id_type=MESH)
    loads = [
        pltpu.make_async_copy(source, target, load_sem.at[i])
        for i, (source, target) in enumerate(
            [
                (ids_in, ids.at[OWN]),
                (params_in, owned.at[0]),
                (damping_in, owned_damping.at[0]),
                (lift_in, lift_b),
                (w_in, w),
                (hw_in, hw_b),
                (targets_in, targets),
                (quad_in, quad_b),
                (enc_in, enc),
            ]
        )
    ]
    for load in loads:
        load.start()

    reply[...] = jnp.zeros_like(reply)
    reply_damping[...] = jnp.zeros_like(reply_damping)
    lift[...] = jnp.zeros_like(lift)
    depth = (lax.broadcasted_iota(jnp.int32, (SAMPLES, D), 0).astype(F) + 1.0) / SAMPLES
    loads[0].wait()
    loads[1].wait()
    pl.semaphore_wait(barrier, len(ANSWERED) + len(LINE))

    for i in ANSWERED:
        send(ids.at[OWN], ids.at[i], 0, PLANE[i])
    for o in LINE:
        send(owned.at[0], owned.at[o[3]], 1, o)
    loads[2].wait()
    for o in LINE:
        send(owned_damping.at[0], owned_damping.at[o[3]], 2, o)
    for load in loads[3:8]:
        load.wait()
    lift[0:PARAMS] = lift_b[...]
    lift2[...] = two_terms(lift[...], 0)
    quad[...] = jnp.broadcast_to(quad_b[...], (D, SAMPLES)).T
    hw = hw_b[...].astype(F)
    for layer in range(LAYERS):
        wt[layer] = w[layer].T

    def terms_of(held):
        wide = jnp.concatenate([held[t] for t in range(4)], axis=1)
        return three_terms(jnp.concatenate([wide, jnp.zeros((2, 4 * COLS), F)], axis=0))

    wait(owned.at[pl.ds(1, 3)], recv_sem.at[1])
    terms = terms_of(owned)
    wait(ids.at[pl.ds(0, ASKERS - 1)], recv_sem.at[0])

    asked = ids[...].reshape(ASKERS, RAYS).astype(F)
    here = lax.broadcasted_iota(jnp.int32, (ASKERS, RAYS), 0) == lax.broadcasted_iota(
        jnp.int32, (ASKERS, RAYS), 1
    )
    asked = jnp.sum(jnp.where(here, asked, 0.0), axis=0, keepdims=True)
    count = lax.broadcasted_iota(jnp.int32, (COLS, RAYS), 0).astype(F)
    picked = []
    for t in range(4):
        cam, ray = device((0, 0, 0, (4 - t) % 4))
        first = ((cam * 16 + ray) * COLS).astype(F)
        picked.append((asked - first == count).astype(B))
    picked = jnp.concatenate(picked, axis=0)

    def answer(terms, rows, landing, n):
        got = dot_terms(terms, picked, ((1,), (0,)))
        rows[:, 0, 0:40] = got.T[0:ASKERS]
        for i in ANSWERED:
            send(rows.at[i], landing.at[i], n, opposite(PLANE[i]))
        landing[OWN] = rows[OWN]

    answer(terms, reply, columns, 3)
    wait(owned_damping.at[pl.ds(1, 3)], recv_sem.at[2])
    answer(terms_of(owned_damping), reply_damping, columns_damping, 4)
    wait(columns.at[pl.ds(0, ASKERS - 1)], recv_sem.at[3])
    column = jnp.sum(columns[...].reshape(ASKERS, D), axis=0, keepdims=True)
    lifted = dot(jnp.broadcast_to(column, (8, D)), lift[...], ((1,), (0,)))[0:1]
    loads[8].wait()
    mlp(enc, depth * lifted, w, wt, hw, quad[...], depth, grads, mixed)

    wait(columns_damping.at[pl.ds(0, ASKERS - 1)], recv_sem.at[4])
    damp = jnp.sum(columns_damping[...].reshape(ASKERS, D), axis=0, keepdims=True)
    residual = dot(hw, mixed[...], ((1,), (1,))) - targets[...]
    lane8 = lax.broadcasted_iota(jnp.int32, (8, D), 1)
    sub8 = lax.broadcasted_iota(jnp.int32, (8, D), 0)
    rows = dot_two(two_terms(grads[...].reshape(COLORS * RAYS, D), 0), lift2[...], ((1,), (1,)))
    residual = jnp.concatenate([residual[c : c + 1] for c in range(COLORS)], axis=1)
    left = jnp.concatenate([rows.T[0:40], jnp.broadcast_to(-residual, (8, COLORS * RAYS))], axis=0)
    matrix = dot_two(two_terms(left, 0), two_terms(rows, 1), ((1,), (0,)))
    right = matrix[40:48]
    camera = ids[OWN][:, 0:1].astype(F)
    damp = jnp.where(lane8 == PARAMS, camera, jnp.broadcast_to(damp, (8, D)))
    out = jnp.zeros((8, D), F)
    for a in range(5):
        moved = matrix[8 * a : 8 * a + 8]
        if a:
            moved = pltpu.roll(moved, OFFS[a] - 8 * a, axis=1)
        inside = (lane8 >= OFFS[a]) & (lane8 < OFFS[a] + 40 - 8 * a)
        out = jnp.where(inside, moved, out)
    for value, sub, first, start in (
        [(right, m, 8 * m, 120) for m in range(5)]
        + [(damp, 5 + m, 8 * m, 120) for m in range(3)]
        + [(damp, 6, 24, 112), (damp, 7, 32, 112)]
    ):
        moved = pltpu.roll(value, start - first, axis=1)
        inside = (sub8 == sub) & (lane8 >= start) & (lane8 < start + 8)
        out = jnp.where(inside, moved, out)
    tiles[HALF - 1] = out
    for g in (2, 1, 0):
        for i in GROUPS[g]:
            send(tiles.at[HALF - 1], tiles.at[i], 5, SAME[i], group_sem.at[g])
    for g in range(3):
        at, n = GROUPS[g][0], len(GROUPS[g])
        wait(tiles.at[pl.ds(at, n)], group_sem.at[g])
        n += g == 0
        send(tiles.at[pl.ds(at, n)], tiles.at[pl.ds(HALF + at, n)], 6, PAIR)
    wait(tiles.at[pl.ds(HALF, HALF)], recv_sem.at[6])

    for r in range(8):
        turned[r] = tiles[:, r, :].T
    rhs = jnp.concatenate([turned[m, 120:128] for m in range(5)], axis=0)
    damping = jnp.concatenate(
        [turned[5, 120:128], turned[6, 120:128], turned[7, 120:128], turned[6, 112:120],
         turned[7, 112:120]], axis=0,
    )
    id_lanes = damping[PARAMS : PARAMS + 1]
    row40 = lax.broadcasted_iota(jnp.int32, (40, N), 0)
    damping = jnp.where(row40 < PARAMS, damping, 0.0)
    id_subs = tiles[:, 7, 112 + 6 : 112 + 7]
    same = id_subs == id_lanes
    earlier = lax.broadcasted_iota(jnp.int32, (N, N), 0) < lax.broadcasted_iota(jnp.int32, (N, N), 1)
    repeats = jnp.sum(jnp.where(same & earlier, 1.0, 0.0), axis=0, keepdims=True)
    once = jnp.where(repeats == 0.0, 1.0, 0.0)
    same = same.astype(B)

    def total(v):
        return jnp.sum(jnp.sum(v * once, axis=0, keepdims=True), axis=1, keepdims=True)

    def operator(v):
        product = matvec(turned, [v[8 * a : 8 * a + 8] for a in range(5)])
        return dot_ones(jnp.concatenate(product, axis=0), same, ((1,), (0,))) + damping * v

    remainder = dot_ones(rhs, same, ((1,), (0,)))
    direction = remainder
    norm = total(remainder * remainder)
    answered = jnp.zeros_like(remainder)
    for it in range(CG_ITERS):
        image = operator(direction)
        step = norm / total(direction * image)
        answered = answered + step * direction
        remainder = remainder - step * image
        if it + 1 < CG_ITERS:
            norm_next = total(remainder * remainder)
            direction = remainder + (norm_next / norm) * direction
            norm = norm_next
    result_out[0:40] = answered * once
    result_out[40:80] = remainder * once
    result_out[80:88] = jnp.broadcast_to(id_lanes, (8, N))
    wait(ids.at[pl.ds(0, ASKERS - 1)], send_sem.at[0])
    wait(owned.at[pl.ds(1, 3)], send_sem.at[1])
    wait(owned_damping.at[pl.ds(1, 3)], send_sem.at[2])
    wait(columns.at[pl.ds(0, ASKERS - 1)], send_sem.at[3])
    wait(columns_damping.at[pl.ds(0, ASKERS - 1)], send_sem.at[4])
    wait(tiles.at[pl.ds(0, HALF - 1)], send_sem.at[5])
    wait(tiles.at[pl.ds(HALF, HALF)], send_sem.at[6])


def place(result, update_out, residual_out):
    first = ((lax.axis_index("cam") * 16 + lax.axis_index("ray")) * COLS).astype(F)
    count = lax.broadcasted_iota(jnp.int32, (COLS, N), 0).astype(F)
    where = (result[80:81] - first == count).astype(B)
    out = dot_ones(result[0:80], where, ((1,), (1,)))
    update_out[...] = out[0:PARAMS]
    residual_out[...] = out[40 : 40 + PARAMS]


def body(encodings, ray_camera, targets, weights, head_weight, quadrature, lift, cam_params, damping):
    vmem = pl.BlockSpec(memory_space=pltpu.VMEM)
    hbm = pl.BlockSpec(memory_space=pl.ANY)
    inputs = (
        quadrature.reshape(1, SAMPLES), ray_camera.reshape(1, RAYS), encodings, targets.T, weights,
        head_weight.T, lift, cam_params, damping,
    )
    result = pl.pallas_call(
        kernel,
        out_shape=jax.ShapeDtypeStruct((88, N), F),
        in_specs=[hbm] * 9,
        out_specs=vmem,
        scratch_shapes=[
            pltpu.VMEM((RAYS, SAMPLES, D), B),
            pltpu.VMEM((COLORS, RAYS), F),
            pltpu.VMEM((LAYERS, D, D), B),
            pltpu.VMEM((COLORS, D), B),
            pltpu.VMEM((PARAMS, D), F),
            pltpu.VMEM((1, SAMPLES), F),
            pltpu.VMEM((LAYERS, D, D), B),
            pltpu.VMEM((D, D), F),
            pltpu.VMEM((2 * D, D), B),
            pltpu.VMEM((SAMPLES, D), F),
            pltpu.VMEM((ASKERS, 1, RAYS), jnp.int32),
            pltpu.VMEM((4, PARAMS, COLS), F),
            pltpu.VMEM((4, PARAMS, COLS), F),
            pltpu.VMEM((ASKERS, 1, D), F),
            pltpu.VMEM((ASKERS, 1, D), F),
            pltpu.VMEM((ASKERS, 1, D), F),
            pltpu.VMEM((ASKERS, 1, D), F),
            pltpu.VMEM((COLORS, RAYS, D), F),
            pltpu.VMEM((RAYS, D), F),
            pltpu.VMEM((N, 8, D), F),
            pltpu.VMEM((8, D, N), F),
            pltpu.SemaphoreType.DMA((9,)),
            pltpu.SemaphoreType.DMA((8,)),
            pltpu.SemaphoreType.DMA((8,)),
            pltpu.SemaphoreType.DMA((3,)),
        ],
        name="pose_solve",
        compiler_params=pltpu.CompilerParams(
            collective_id=0, has_side_effects=True, vmem_limit_bytes=48 * 2**20
        ),
    )(
        *(pltpu.with_memory_space_constraint(x, pltpu.HBM) for x in inputs)
    )
    out = jax.ShapeDtypeStruct((PARAMS, COLS), F)
    return pl.pallas_call(
        place, out_shape=(out, out), in_specs=[vmem], out_specs=(vmem, vmem), name="pose_place",
        compiler_params=pltpu.CompilerParams(vmem_limit_bytes=8 * 2**20),
    )(result)


def solution(mesh):
    in_specs = (
        P(BOTH, None, None), P(BOTH), P(BOTH, None), P(), P(), P(), P(), P(None, BOTH), P(None, BOTH),
    )
    out_specs = (P(None, BOTH), P(None, BOTH))
    return jax.shard_map(body, mesh=mesh, in_specs=in_specs, out_specs=out_specs, check_vma=False)
```

```python
import functools

import jax
import jax.numpy as jnp
from jax import lax
from jax.experimental import pallas as pl
from jax.experimental.pallas import tpu as pltpu
from jax.sharding import PartitionSpec as P

F = jnp.float32
B = jnp.bfloat16
MESH = pl.DeviceIdType.MESH
BOTH = ("cam", "ray")
N = 128
D = 128
SAMPLES = 48
COLORS = 3
RAYS = 64
LAYERS = 4
PARAMS = 38
COLS = 256
CG_ITERS = 2
STEP_RAYS = 64
HI = lax.Precision.HIGHEST
OFFS = (0, 40, 72, 96, 112)


def far(o):
    return sum(min(d, 4 - d) for d in (o[0], o[2], o[3]))


OTHERS = sorted(
    (
        (dz, dc, dy, dx)
        for dz in range(4)
        for dc in range(2)
        for dy in range(4)
        for dx in range(4)
        if (dz, dc, dy, dx) != (0, 0, 0, 0)
    ),
    key=lambda o: -far(o),
)
ROW = [(dc, dy) for dc, dy in ((0, 2), (1, 2), (0, 1), (0, 3), (1, 1), (1, 3), (1, 0), (0, 0))]
PLANE = [(dz, dc, dy, 0) for dz in range(4) for dc, dy in ROW]
OWN = len(ROW) - 1
ROWS = [(0, dc, dy, 0) for dc, dy in ROW[:OWN]]
COLUMN = [(dz, 0, 0, 0) for dz in (2, 1, 3)]
LINE = [(0, 0, 0, dx) for dx in (2, 1, 3)]
SAME = [o for o in OTHERS if o[1] == 0]
PAIR = (0, 1, 0, 0)
ANSWERED = sorted((i for i in range(len(PLANE)) if i != OWN), key=lambda i: -far(PLANE[i]))
ASKERS = len(PLANE)
HALF = len(SAME) + 1
GROUPS = [[i for i, o in enumerate(SAME) if far(o) in hops] for hops in ((1, 2), (3,), (4, 5, 6))]


def device(o):
    cam, ray = lax.axis_index("cam"), lax.axis_index("ray")
    z, c, y, x = cam // 2, cam % 2, ray // 4, ray % 4
    return (z + o[0]) % 4 * 2 + (c + o[1]) % 2, (y + o[2]) % 4 * 4 + (x + o[3]) % 4


def opposite(o):
    return (-o[0]) % 4, (-o[1]) % 2, (-o[2]) % 4, (-o[3]) % 4


def dot(a, b, dims, precision=HI):
    return lax.dot_general(a, b, (dims, ((), ())), precision=precision, preferred_element_type=F)


def three_terms(a):
    high = a.astype(B)
    rest = a - high.astype(F)
    middle = rest.astype(B)
    low = (rest - middle.astype(F)).astype(B)
    return jnp.concatenate([high, middle, low], axis=0)


def two_terms(a, axis):
    high = a.astype(B)
    return jnp.concatenate([high, (a - high.astype(F)).astype(B)], axis=axis)


def dot_two(a, b, dims):
    out = dot(a, b, dims, None)
    m, n = out.shape[0] // 2, out.shape[1] // 2
    return (out[0:m, 0:n] + (out[0:m, n:] + out[m:, 0:n])) + out[m:, n:]


def dot_terms(terms, b, dims):
    n = terms.shape[0] // 3
    out = dot(terms, b, dims, None)
    return out[0:n] + out[n : 2 * n] + out[2 * n : 3 * n]


def dot_ones(a, b, dims):
    return dot_terms(three_terms(a), b, dims)


def mlp(enc, de, w, wt, hw, quad, depth, grads, mixed):
    rows = STEP_RAYS * SAMPLES
    quad, depth = quad[None], depth[None]

    def step(t, carry):
        at = pl.ds(pl.multiple_of(t * STEP_RAYS, STEP_RAYS), STEP_RAYS)
        h = jnp.tanh(enc[at].astype(F) + de[None]).astype(B).reshape(rows, D)
        hs = [h]
        for layer in range(LAYERS):
            h = jnp.tanh(jnp.dot(h, w[layer], preferred_element_type=F)).astype(B)
            hs.append(h)
        last = h.astype(F).reshape(STEP_RAYS, SAMPLES, D)
        mixed[at] = jnp.sum(quad * last, axis=1)
        slope = ((1.0 - last * last) * quad).reshape(rows, D)
        ys = [(slope * hw[c : c + 1]).astype(B) for c in range(COLORS)]
        for layer in range(LAYERS - 1, 0, -1):
            inner = hs[layer].astype(F)
            slope = 1.0 - inner * inner
            ys = [(jnp.dot(y, wt[layer], preferred_element_type=F) * slope).astype(B) for y in ys]
        first = hs[0].astype(F).reshape(STEP_RAYS, SAMPLES, D)
        slope = (1.0 - first * first) * depth
        for c in range(COLORS):
            inner = jnp.dot(ys[c], wt[0], preferred_element_type=F)
            grads[c, at] = jnp.sum(inner.reshape(STEP_RAYS, SAMPLES, D) * slope, axis=1)
        return carry

    lax.fori_loop(0, RAYS // STEP_RAYS, step, 0)


def matvec(turned, v):
    sub = lax.broadcasted_iota(jnp.int32, (8, N), 0)
    outs = [jnp.zeros((8, N), F) for _ in range(5)]
    for r in range(8):
        for a in range(5):
            if 8 * a + r >= PARAMS:
                continue
            own = v[a][r : r + 1]
            total = None
            for j in range(a, 5):
                at = OFFS[a] + 8 * (j - a)
                piece = turned[r, at : at + 8]
                term = piece * v[j]
                total = term if total is None else total + term
                if j > a:
                    outs[j] = outs[j] + piece * own
            row = jnp.sum(total, axis=0, keepdims=True)
            outs[a] = outs[a] + jnp.where(sub == r, row, 0.0)
    return outs


def kernel(
    quad_in, ids_in, enc_in, targets_in, w_in, hw_in, lift_in, params_in, damping_in,
    result_out,
    enc, targets, w, hw_b, lift_b, quad_b, wt, lift, lift2, quad, ids, owned, owned_damping,
    reply, reply_damping, columns, columns_damping, grads, mixed, tiles, turned,
    load_sem, send_sem, recv_sem, group_sem,
):
    def send(source, target, n, o, recv=None):
        pltpu.make_async_remote_copy(
            source, target, send_sem.at[n], recv_sem.at[n] if recv is None else recv,
            device_id=device(o), device_id_type=MESH,
        ).start()

    def wait(ref, sem):
        pltpu.make_async_copy(ref, ref, sem).wait()

    barrier = pltpu.get_barrier_semaphore()
    for o in [opposite(PLANE[i]) for i in ANSWERED] + LINE:
        pl.semaphore_signal(barrier, inc=1, device_id=device(o), device_id_type=MESH)
    loads = [
        pltpu.make_async_copy(source, target, load_sem.at[i])
        for i, (source, target) in enumerate(
            [
                (ids_in, ids.at[OWN]),
                (params_in, owned.at[0]),
                (damping_in, owned_damping.at[0]),
                (lift_in, lift_b),
                (w_in, w),
                (hw_in, hw_b),
                (targets_in, targets),
                (quad_in, quad_b),
                (enc_in, enc),
            ]
        )
    ]
    for load in loads:
        load.start()

    reply[...] = jnp.zeros_like(reply)
    reply_damping[...] = jnp.zeros_like(reply_damping)
    lift[...] = jnp.zeros_like(lift)
    depth = (lax.broadcasted_iota(jnp.int32, (SAMPLES, D), 0).astype(F) + 1.0) / SAMPLES
    loads[0].wait()
    loads[1].wait()
    pl.semaphore_wait(barrier, len(ANSWERED) + len(LINE))

    for i in ANSWERED:
        send(ids.at[OWN], ids.at[i], 0, PLANE[i])
    for o in LINE:
        send(owned.at[0], owned.at[o[3]], 1, o)
    for load in loads[2:8]:
        load.wait()
    lift[0:PARAMS] = lift_b[...]
    lift2[...] = two_terms(lift[...], 0)
    quad[...] = jnp.broadcast_to(quad_b[...], (D, SAMPLES)).T
    hw = hw_b[...].astype(F)
    for layer in range(LAYERS):
        wt[layer] = w[layer].T

    def terms_of(held):
        wide = jnp.concatenate([held[t] for t in range(4)], axis=1)
        return three_terms(jnp.concatenate([wide, jnp.zeros((2, 4 * COLS), F)], axis=0))

    wait(owned.at[pl.ds(1, 3)], recv_sem.at[1])
    for o in LINE:
        send(owned_damping.at[0], owned_damping.at[o[3]], 2, o)
    terms = terms_of(owned)
    wait(ids.at[pl.ds(0, ASKERS - 1)], recv_sem.at[0])

    asked = ids[...].reshape(ASKERS, RAYS).astype(F)
    here = lax.broadcasted_iota(jnp.int32, (ASKERS, RAYS), 0) == lax.broadcasted_iota(
        jnp.int32, (ASKERS, RAYS), 1
    )
    asked = jnp.sum(jnp.where(here, asked, 0.0), axis=0, keepdims=True)
    count = lax.broadcasted_iota(jnp.int32, (COLS, RAYS), 0).astype(F)
    picked = []
    for t in range(4):
        cam, ray = device((0, 0, 0, (4 - t) % 4))
        first = ((cam * 16 + ray) * COLS).astype(F)
        picked.append((asked - first == count).astype(B))
    picked = jnp.concatenate(picked, axis=0)

    def answer(terms, rows, landing, n):
        got = dot_terms(terms, picked, ((1,), (0,)))
        rows[:, 0, 0:40] = got.T[0:ASKERS]
        for i in ANSWERED:
            send(rows.at[i], landing.at[i], n, opposite(PLANE[i]))
        landing[OWN] = rows[OWN]

    answer(terms, reply, columns, 3)
    wait(owned_damping.at[pl.ds(1, 3)], recv_sem.at[2])
    answer(terms_of(owned_damping), reply_damping, columns_damping, 4)
    wait(columns.at[pl.ds(0, ASKERS - 1)], recv_sem.at[3])
    column = jnp.sum(columns[...].reshape(ASKERS, D), axis=0, keepdims=True)
    lifted = dot(jnp.broadcast_to(column, (8, D)), lift[...], ((1,), (0,)))[0:1]
    loads[8].wait()
    mlp(enc, depth * lifted, w, wt, hw, quad[...], depth, grads, mixed)

    wait(columns_damping.at[pl.ds(0, ASKERS - 1)], recv_sem.at[4])
    damp = jnp.sum(columns_damping[...].reshape(ASKERS, D), axis=0, keepdims=True)
    residual = dot(hw, mixed[...], ((1,), (1,))) - targets[...]
    lane8 = lax.broadcasted_iota(jnp.int32, (8, D), 1)
    sub8 = lax.broadcasted_iota(jnp.int32, (8, D), 0)
    rows = dot_two(two_terms(grads[...].reshape(COLORS * RAYS, D), 0), lift2[...], ((1,), (1,)))
    residual = jnp.concatenate([residual[c : c + 1] for c in range(COLORS)], axis=1)
    left = jnp.concatenate([rows.T[0:40], jnp.broadcast_to(-residual, (8, COLORS * RAYS))], axis=0)
    matrix = dot_two(two_terms(left, 0), two_terms(rows, 1), ((1,), (0,)))
    right = matrix[40:48]
    camera = ids[OWN][:, 0:1].astype(F)
    damp = jnp.where(lane8 == PARAMS, camera, jnp.broadcast_to(damp, (8, D)))
    out = jnp.zeros((8, D), F)
    for a in range(5):
        moved = matrix[8 * a : 8 * a + 8]
        if a:
            moved = pltpu.roll(moved, OFFS[a] - 8 * a, axis=1)
        inside = (lane8 >= OFFS[a]) & (lane8 < OFFS[a] + 40 - 8 * a)
        out = jnp.where(inside, moved, out)
    for value, sub, first, start in (
        [(right, m, 8 * m, 120) for m in range(5)]
        + [(damp, 5 + m, 8 * m, 120) for m in range(3)]
        + [(damp, 6, 24, 112), (damp, 7, 32, 112)]
    ):
        moved = pltpu.roll(value, start - first, axis=1)
        inside = (sub8 == sub) & (lane8 >= start) & (lane8 < start + 8)
        out = jnp.where(inside, moved, out)
    tiles[HALF - 1] = out
    for g in (2, 1, 0):
        for i in GROUPS[g]:
            send(tiles.at[HALF - 1], tiles.at[i], 5, SAME[i], group_sem.at[g])
    for g in range(3):
        at, n = GROUPS[g][0], len(GROUPS[g])
        wait(tiles.at[pl.ds(at, n)], group_sem.at[g])
        n += g == 0
        send(tiles.at[pl.ds(at, n)], tiles.at[pl.ds(HALF + at, n)], 6, PAIR)
    wait(tiles.at[pl.ds(HALF, HALF)], recv_sem.at[6])

    for r in range(8):
        turned[r] = tiles[:, r, :].T
    rhs = jnp.concatenate([turned[m, 120:128] for m in range(5)], axis=0)
    damping = jnp.concatenate(
        [turned[5, 120:128], turned[6, 120:128], turned[7, 120:128], turned[6, 112:120],
         turned[7, 112:120]], axis=0,
    )
    id_lanes = damping[PARAMS : PARAMS + 1]
    row40 = lax.broadcasted_iota(jnp.int32, (40, N), 0)
    damping = jnp.where(row40 < PARAMS, damping, 0.0)
    id_subs = tiles[:, 7, 112 + 6 : 112 + 7]
    same = id_subs == id_lanes
    earlier = lax.broadcasted_iota(jnp.int32, (N, N), 0) < lax.broadcasted_iota(jnp.int32, (N, N), 1)
    repeats = jnp.sum(jnp.where(same & earlier, 1.0, 0.0), axis=0, keepdims=True)
    once = jnp.where(repeats == 0.0, 1.0, 0.0)
    same = same.astype(B)

    def total(v):
        return jnp.sum(jnp.sum(v * once, axis=0, keepdims=True), axis=1, keepdims=True)

    def operator(v):
        product = matvec(turned, [v[8 * a : 8 * a + 8] for a in range(5)])
        return dot_ones(jnp.concatenate(product, axis=0), same, ((1,), (0,))) + damping * v

    remainder = dot_ones(rhs, same, ((1,), (0,)))
    direction = remainder
    norm = total(remainder * remainder)
    answered = jnp.zeros_like(remainder)
    for it in range(CG_ITERS):
        image = operator(direction)
        step = norm / total(direction * image)
        answered = answered + step * direction
        remainder = remainder - step * image
        if it + 1 < CG_ITERS:
            norm_next = total(remainder * remainder)
            direction = remainder + (norm_next / norm) * direction
            norm = norm_next
    result_out[0:40] = answered * once
    result_out[40:80] = remainder * once
    result_out[80:88] = jnp.broadcast_to(id_lanes, (8, N))
    wait(ids.at[pl.ds(0, ASKERS - 1)], send_sem.at[0])
    wait(owned.at[pl.ds(1, 3)], send_sem.at[1])
    wait(owned_damping.at[pl.ds(1, 3)], send_sem.at[2])
    wait(columns.at[pl.ds(0, ASKERS - 1)], send_sem.at[3])
    wait(columns_damping.at[pl.ds(0, ASKERS - 1)], send_sem.at[4])
    wait(tiles.at[pl.ds(0, HALF - 1)], send_sem.at[5])
    wait(tiles.at[pl.ds(HALF, HALF)], send_sem.at[6])


def place(result, update_out, residual_out):
    first = ((lax.axis_index("cam") * 16 + lax.axis_index("ray")) * COLS).astype(F)
    count = lax.broadcasted_iota(jnp.int32, (COLS, N), 0).astype(F)
    where = (result[80:81] - first == count).astype(B)
    out = dot_ones(result[0:80], where, ((1,), (1,)))
    update_out[...] = out[0:PARAMS]
    residual_out[...] = out[40 : 40 + PARAMS]


def body(encodings, ray_camera, targets, weights, head_weight, quadrature, lift, cam_params, damping):
    vmem = pl.BlockSpec(memory_space=pltpu.VMEM)
    hbm = pl.BlockSpec(memory_space=pl.ANY)
    inputs = (
        quadrature.reshape(1, SAMPLES), ray_camera.reshape(1, RAYS), encodings, targets.T, weights,
        head_weight.T, lift, cam_params, damping,
    )
    result = pl.pallas_call(
        kernel,
        out_shape=jax.ShapeDtypeStruct((88, N), F),
        in_specs=[hbm] * 9,
        out_specs=vmem,
        scratch_shapes=[
            pltpu.VMEM((RAYS, SAMPLES, D), B),
            pltpu.VMEM((COLORS, RAYS), F),
            pltpu.VMEM((LAYERS, D, D), B),
            pltpu.VMEM((COLORS, D), B),
            pltpu.VMEM((PARAMS, D), F),
            pltpu.VMEM((1, SAMPLES), F),
            pltpu.VMEM((LAYERS, D, D), B),
            pltpu.VMEM((D, D), F),
            pltpu.VMEM((2 * D, D), B),
            pltpu.VMEM((SAMPLES, D), F),
            pltpu.VMEM((ASKERS, 1, RAYS), jnp.int32),
            pltpu.VMEM((4, PARAMS, COLS), F),
            pltpu.VMEM((4, PARAMS, COLS), F),
            pltpu.VMEM((ASKERS, 1, D), F),
            pltpu.VMEM((ASKERS, 1, D), F),
            pltpu.VMEM((ASKERS, 1, D), F),
            pltpu.VMEM((ASKERS, 1, D), F),
            pltpu.VMEM((COLORS, RAYS, D), F),
            pltpu.VMEM((RAYS, D), F),
            pltpu.VMEM((N, 8, D), F),
            pltpu.VMEM((8, D, N), F),
            pltpu.SemaphoreType.DMA((9,)),
            pltpu.SemaphoreType.DMA((8,)),
            pltpu.SemaphoreType.DMA((8,)),
            pltpu.SemaphoreType.DMA((3,)),
        ],
        name="pose_solve",
        compiler_params=pltpu.CompilerParams(
            collective_id=0, has_side_effects=True, vmem_limit_bytes=48 * 2**20
        ),
    )(
        *(pltpu.with_memory_space_constraint(x, pltpu.HBM) for x in inputs)
    )
    out = jax.ShapeDtypeStruct((PARAMS, COLS), F)
    return pl.pallas_call(
        place, out_shape=(out, out), in_specs=[vmem], out_specs=(vmem, vmem), name="pose_place",
        compiler_params=pltpu.CompilerParams(vmem_limit_bytes=8 * 2**20),
    )(result)


def solution(mesh):
    in_specs = (
        P(BOTH, None, None), P(BOTH), P(BOTH, None), P(), P(), P(), P(), P(None, BOTH), P(None, BOTH),
    )
    out_specs = (P(None, BOTH), P(None, BOTH))
    return jax.shard_map(body, mesh=mesh, in_specs=in_specs, out_specs=out_specs, check_vma=False)
```

```python
import functools

import jax
import jax.numpy as jnp
from jax import lax
from jax.experimental import pallas as pl
from jax.experimental.pallas import tpu as pltpu
from jax.sharding import PartitionSpec as P

F = jnp.float32
B = jnp.bfloat16
MESH = pl.DeviceIdType.MESH
BOTH = ("cam", "ray")
N = 128
D = 128
SAMPLES = 48
COLORS = 3
RAYS = 64
LAYERS = 4
PARAMS = 38
COLS = 256
CG_ITERS = 2
STEP_RAYS = 64
HI = lax.Precision.HIGHEST
OFFS = (0, 40, 72, 96, 112)


def far(o):
    return sum(min(d, 4 - d) for d in (o[0], o[2], o[3]))


OTHERS = sorted(
    (
        (dz, dc, dy, dx)
        for dz in range(4)
        for dc in range(2)
        for dy in range(4)
        for dx in range(4)
        if (dz, dc, dy, dx) != (0, 0, 0, 0)
    ),
    key=lambda o: -far(o),
)
ROW = [(dc, dy) for dc, dy in ((0, 2), (1, 2), (0, 1), (0, 3), (1, 1), (1, 3), (1, 0), (0, 0))]
PLANE = [(dz, dc, dy, 0) for dz in range(4) for dc, dy in ROW]
OWN = len(ROW) - 1
ROWS = [(0, dc, dy, 0) for dc, dy in ROW[:OWN]]
COLUMN = [(dz, 0, 0, 0) for dz in (2, 1, 3)]
LINE = [(0, 0, 0, dx) for dx in (2, 1, 3)]
SAME = [o for o in OTHERS if o[1] == 0]
PAIR = (0, 1, 0, 0)
ANSWERED = sorted((i for i in range(len(PLANE)) if i != OWN), key=lambda i: -far(PLANE[i]))
ASKERS = len(PLANE)
HALF = len(SAME) + 1
GROUPS = [[i for i, o in enumerate(SAME) if far(o) in hops] for hops in ((1, 2), (3,), (4, 5, 6))]


def device(o):
    cam, ray = lax.axis_index("cam"), lax.axis_index("ray")
    z, c, y, x = cam // 2, cam % 2, ray // 4, ray % 4
    return (z + o[0]) % 4 * 2 + (c + o[1]) % 2, (y + o[2]) % 4 * 4 + (x + o[3]) % 4


def opposite(o):
    return (-o[0]) % 4, (-o[1]) % 2, (-o[2]) % 4, (-o[3]) % 4


def dot(a, b, dims, precision=HI):
    return lax.dot_general(a, b, (dims, ((), ())), precision=precision, preferred_element_type=F)


def three_terms(a):
    high = a.astype(B)
    rest = a - high.astype(F)
    middle = rest.astype(B)
    low = (rest - middle.astype(F)).astype(B)
    return jnp.concatenate([high, middle, low], axis=0)


def two_terms(a, axis):
    high = a.astype(B)
    return jnp.concatenate([high, (a - high.astype(F)).astype(B)], axis=axis)


def dot_two(a, b, dims):
    out = dot(a, b, dims, None)
    m, n = out.shape[0] // 2, out.shape[1] // 2
    return (out[0:m, 0:n] + (out[0:m, n:] + out[m:, 0:n])) + out[m:, n:]


def dot_terms(terms, b, dims):
    n = terms.shape[0] // 3
    out = dot(terms, b, dims, None)
    return out[0:n] + out[n : 2 * n] + out[2 * n : 3 * n]


def dot_ones(a, b, dims):
    return dot_terms(three_terms(a), b, dims)


def mlp(enc, de, w, wt, hw, quad, depth, grads, mixed):
    rows = STEP_RAYS * SAMPLES
    quad, depth = quad[None], depth[None]

    def step(t, carry):
        at = pl.ds(pl.multiple_of(t * STEP_RAYS, STEP_RAYS), STEP_RAYS)
        h = jnp.tanh(enc[at].astype(F) + de[None]).astype(B).reshape(rows, D)
        hs = [h]
        for layer in range(LAYERS):
            h = jnp.tanh(jnp.dot(h, w[layer], preferred_element_type=F)).astype(B)
            hs.append(h)
        last = h.astype(F).reshape(STEP_RAYS, SAMPLES, D)
        mixed[at] = jnp.sum(quad * last, axis=1)
        slope = ((1.0 - last * last) * quad).reshape(rows, D)
        ys = [(slope * hw[c : c + 1]).astype(B) for c in range(COLORS)]
        for layer in range(LAYERS - 1, 0, -1):
            inner = hs[layer].astype(F)
            slope = 1.0 - inner * inner
            ys = [(jnp.dot(y, wt[layer], preferred_element_type=F) * slope).astype(B) for y in ys]
        first = hs[0].astype(F).reshape(STEP_RAYS, SAMPLES, D)
        slope = (1.0 - first * first) * depth
        for c in range(COLORS):
            inner = jnp.dot(ys[c], wt[0], preferred_element_type=F)
            grads[c, at] = jnp.sum(inner.reshape(STEP_RAYS, SAMPLES, D) * slope, axis=1)
        return carry

    lax.fori_loop(0, RAYS // STEP_RAYS, step, 0)


def matvec(turned, v):
    sub = lax.broadcasted_iota(jnp.int32, (8, N), 0)
    outs = [jnp.zeros((8, N), F) for _ in range(5)]
    for r in range(8):
        for a in range(5):
            if 8 * a + r >= PARAMS:
                continue
            own = v[a][r : r + 1]
            total = None
            for j in range(a, 5):
                at = OFFS[a] + 8 * (j - a)
                piece = turned[r, at : at + 8]
                term = piece * v[j]
                total = term if total is None else total + term
                if j > a:
                    outs[j] = outs[j] + piece * own
            row = jnp.sum(total, axis=0, keepdims=True)
            outs[a] = outs[a] + jnp.where(sub == r, row, 0.0)
    return outs


def kernel(
    quad_in, ids_in, enc_in, targets_in, w_in, hw_in, lift_in, params_in, damping_in,
    result_out,
    enc, targets, w, hw_b, lift_b, quad_b, wt, lift, lift2, quad, ids, owned, owned_damping,
    reply, reply_damping, columns, columns_damping, grads, mixed, tiles, turned,
    load_sem, send_sem, recv_sem, group_sem,
):
    def send(source, target, n, o, recv=None):
        pltpu.make_async_remote_copy(
            source, target, send_sem.at[n], recv_sem.at[n] if recv is None else recv,
            device_id=device(o), device_id_type=MESH,
        ).start()

    def wait(ref, sem):
        pltpu.make_async_copy(ref, ref, sem).wait()

    barrier = pltpu.get_barrier_semaphore()
    for o in [opposite(PLANE[i]) for i in ANSWERED] + LINE:
        pl.semaphore_signal(barrier, inc=1, device_id=device(o), device_id_type=MESH)
    loads = [
        pltpu.make_async_copy(source, target, load_sem.at[i])
        for i, (source, target) in enumerate(
            [
                (ids_in, ids.at[OWN]),
                (params_in, owned.at[0]),
                (damping_in, owned_damping.at[0]),
                (lift_in, lift_b),
                (w_in, w),
                (hw_in, hw_b),
                (targets_in, targets),
                (quad_in, quad_b),
                (enc_in, enc),
            ]
        )
    ]
    for load in loads:
        load.start()

    reply[...] = jnp.zeros_like(reply)
    reply_damping[...] = jnp.zeros_like(reply_damping)
    lift[...] = jnp.zeros_like(lift)
    depth = (lax.broadcasted_iota(jnp.int32, (SAMPLES, D), 0).astype(F) + 1.0) / SAMPLES
    loads[0].wait()
    loads[1].wait()
    pl.semaphore_wait(barrier, len(ANSWERED) + len(LINE))

    for i in ANSWERED:
        send(ids.at[OWN], ids.at[i], 0, PLANE[i])
    for o in LINE:
        send(owned.at[0], owned.at[o[3]], 1, o)
    for load in loads[2:8]:
        load.wait()
    lift[0:PARAMS] = lift_b[...]
    lift2[...] = two_terms(lift[...], 0)
    quad[...] = jnp.broadcast_to(quad_b[...], (D, SAMPLES)).T
    hw = hw_b[...].astype(F)
    for layer in range(LAYERS):
        wt[layer] = w[layer].T

    def terms_of(held):
        wide = jnp.concatenate([held[t] for t in range(4)], axis=1)
        return three_terms(jnp.concatenate([wide, jnp.zeros((2, 4 * COLS), F)], axis=0))

    wait(owned.at[pl.ds(1, 3)], recv_sem.at[1])
    for o in LINE:
        send(owned_damping.at[0], owned_damping.at[o[3]], 2, o)
    terms = terms_of(owned)
    wait(ids.at[pl.ds(0, ASKERS - 1)], recv_sem.at[0])

    asked = ids[...].reshape(ASKERS, RAYS).astype(F)
    here = lax.broadcasted_iota(jnp.int32, (ASKERS, RAYS), 0) == lax.broadcasted_iota(
        jnp.int32, (ASKERS, RAYS), 1
    )
    asked = jnp.sum(jnp.where(here, asked, 0.0), axis=0, keepdims=True)
    count = lax.broadcasted_iota(jnp.int32, (COLS, RAYS), 0).astype(F)
    picked = []
    for t in range(4):
        cam, ray = device((0, 0, 0, (4 - t) % 4))
        first = ((cam * 16 + ray) * COLS).astype(F)
        picked.append((asked - first == count).astype(B))
    picked = jnp.concatenate(picked, axis=0)

    def answer(terms, rows, landing, n):
        got = dot_terms(terms, picked, ((1,), (0,)))
        rows[:, 0, 0:40] = got.T[0:ASKERS]
        for i in ANSWERED:
            send(rows.at[i], landing.at[i], n, opposite(PLANE[i]))
        landing[OWN] = rows[OWN]

    answer(terms, reply, columns, 3)
    wait(owned_damping.at[pl.ds(1, 3)], recv_sem.at[2])
    answer(terms_of(owned_damping), reply_damping, columns_damping, 4)
    wait(columns.at[pl.ds(0, ASKERS - 1)], recv_sem.at[3])
    column = jnp.sum(columns[...].reshape(ASKERS, D), axis=0, keepdims=True)
    lifted = dot(jnp.broadcast_to(column, (8, D)), lift[...], ((1,), (0,)))[0:1]
    loads[8].wait()
    mlp(enc, depth * lifted, w, wt, hw, quad[...], depth, grads, mixed)

    wait(columns_damping.at[pl.ds(0, ASKERS - 1)], recv_sem.at[4])
    damp = jnp.sum(columns_damping[...].reshape(ASKERS, D), axis=0, keepdims=True)
    residual = dot(hw, mixed[...], ((1,), (1,))) - targets[...]
    lane8 = lax.broadcasted_iota(jnp.int32, (8, D), 1)
    sub8 = lax.broadcasted_iota(jnp.int32, (8, D), 0)
    rows = dot_two(two_terms(grads[...].reshape(COLORS * RAYS, D), 0), lift2[...], ((1,), (1,)))
    residual = jnp.concatenate([residual[c : c + 1] for c in range(COLORS)], axis=1)
    left = jnp.concatenate([rows.T[0:40], jnp.broadcast_to(-residual, (8, COLORS * RAYS))], axis=0)
    matrix = dot_two(two_terms(left, 0), two_terms(rows, 1), ((1,), (0,)))
    right = matrix[40:48]
    camera = ids[OWN][:, 0:1].astype(F)
    damp = jnp.where(lane8 == PARAMS, camera, jnp.broadcast_to(damp, (8, D)))
    out = jnp.zeros((8, D), F)
    for a in range(5):
        moved = matrix[8 * a : 8 * a + 8]
        if a:
            moved = pltpu.roll(moved, OFFS[a] - 8 * a, axis=1)
        inside = (lane8 >= OFFS[a]) & (lane8 < OFFS[a] + 40 - 8 * a)
        out = jnp.where(inside, moved, out)
    for value, sub, first, start in (
        [(right, m, 8 * m, 120) for m in range(5)]
        + [(damp, 5 + m, 8 * m, 120) for m in range(3)]
        + [(damp, 6, 24, 112), (damp, 7, 32, 112)]
    ):
        moved = pltpu.roll(value, start - first, axis=1)
        inside = (sub8 == sub) & (lane8 >= start) & (lane8 < start + 8)
        out = jnp.where(inside, moved, out)
    slots = lambda at, n=1: tiles.at[pl.ds(8 * at, 8 * n)]
    tiles[8 * (HALF - 1) : 8 * HALF] = out
    for g in (2, 1, 0):
        for i in GROUPS[g]:
            send(slots(HALF - 1), slots(i), 5, SAME[i], group_sem.at[g])
    for g in range(3):
        at, n = GROUPS[g][0], len(GROUPS[g])
        wait(slots(at, n), group_sem.at[g])
        n += g == 0
        send(slots(at, n), slots(HALF + at, n), 6, PAIR)
    wait(slots(HALF, HALF), recv_sem.at[6])

    for r in range(8):
        turned[r] = tiles[pl.ds(r, N, stride=8), :].T
    rhs = jnp.concatenate([turned[m, 120:128] for m in range(5)], axis=0)
    damping = jnp.concatenate(
        [turned[5, 120:128], turned[6, 120:128], turned[7, 120:128], turned[6, 112:120],
         turned[7, 112:120]], axis=0,
    )
    id_lanes = damping[PARAMS : PARAMS + 1]
    row40 = lax.broadcasted_iota(jnp.int32, (40, N), 0)
    damping = jnp.where(row40 < PARAMS, damping, 0.0)
    id_subs = tiles[pl.ds(7, N, stride=8), :][:, 112 + 6 : 112 + 7]
    same = id_subs == id_lanes
    earlier = lax.broadcasted_iota(jnp.int32, (N, N), 0) < lax.broadcasted_iota(jnp.int32, (N, N), 1)
    repeats = jnp.sum(jnp.where(same & earlier, 1.0, 0.0), axis=0, keepdims=True)
    once = jnp.where(repeats == 0.0, 1.0, 0.0)
    same = same.astype(B)

    def total(v):
        return jnp.sum(jnp.sum(v * once, axis=0, keepdims=True), axis=1, keepdims=True)

    def operator(v):
        product = matvec(turned, [v[8 * a : 8 * a + 8] for a in range(5)])
        return dot_ones(jnp.concatenate(product, axis=0), same, ((1,), (0,))) + damping * v

    remainder = dot_ones(rhs, same, ((1,), (0,)))
    direction = remainder
    norm = total(remainder * remainder)
    answered = jnp.zeros_like(remainder)
    for it in range(CG_ITERS):
        image = operator(direction)
        step = norm / total(direction * image)
        answered = answered + step * direction
        remainder = remainder - step * image
        if it + 1 < CG_ITERS:
            norm_next = total(remainder * remainder)
            direction = remainder + (norm_next / norm) * direction
            norm = norm_next
    result_out[0:40] = answered * once
    result_out[40:80] = remainder * once
    result_out[80:88] = jnp.broadcast_to(id_lanes, (8, N))
    wait(ids.at[pl.ds(0, ASKERS - 1)], send_sem.at[0])
    wait(owned.at[pl.ds(1, 3)], send_sem.at[1])
    wait(owned_damping.at[pl.ds(1, 3)], send_sem.at[2])
    wait(columns.at[pl.ds(0, ASKERS - 1)], send_sem.at[3])
    wait(columns_damping.at[pl.ds(0, ASKERS - 1)], send_sem.at[4])
    wait(slots(0, HALF - 1), send_sem.at[5])
    wait(slots(HALF, HALF), send_sem.at[6])


def place(result, update_out, residual_out):
    first = ((lax.axis_index("cam") * 16 + lax.axis_index("ray")) * COLS).astype(F)
    count = lax.broadcasted_iota(jnp.int32, (COLS, N), 0).astype(F)
    where = (result[80:81] - first == count).astype(B)
    out = dot_ones(result[0:80], where, ((1,), (1,)))
    update_out[...] = out[0:PARAMS]
    residual_out[...] = out[40 : 40 + PARAMS]


def body(encodings, ray_camera, targets, weights, head_weight, quadrature, lift, cam_params, damping):
    vmem = pl.BlockSpec(memory_space=pltpu.VMEM)
    hbm = pl.BlockSpec(memory_space=pl.ANY)
    inputs = (
        quadrature.reshape(1, SAMPLES), ray_camera.reshape(1, RAYS), encodings, targets.T, weights,
        head_weight.T, lift, cam_params, damping,
    )
    result = pl.pallas_call(
        kernel,
        out_shape=jax.ShapeDtypeStruct((88, N), F),
        in_specs=[hbm] * 9,
        out_specs=vmem,
        scratch_shapes=[
            pltpu.VMEM((RAYS, SAMPLES, D), B),
            pltpu.VMEM((COLORS, RAYS), F),
            pltpu.VMEM((LAYERS, D, D), B),
            pltpu.VMEM((COLORS, D), B),
            pltpu.VMEM((PARAMS, D), F),
            pltpu.VMEM((1, SAMPLES), F),
            pltpu.VMEM((LAYERS, D, D), B),
            pltpu.VMEM((D, D), F),
            pltpu.VMEM((2 * D, D), B),
            pltpu.VMEM((SAMPLES, D), F),
            pltpu.VMEM((ASKERS, 1, RAYS), jnp.int32),
            pltpu.VMEM((4, PARAMS, COLS), F),
            pltpu.VMEM((4, PARAMS, COLS), F),
            pltpu.VMEM((ASKERS, 1, D), F),
            pltpu.VMEM((ASKERS, 1, D), F),
            pltpu.VMEM((ASKERS, 1, D), F),
            pltpu.VMEM((ASKERS, 1, D), F),
            pltpu.VMEM((COLORS, RAYS, D), F),
            pltpu.VMEM((RAYS, D), F),
            pltpu.VMEM((N * 8, D), F),
            pltpu.VMEM((8, D, N), F),
            pltpu.SemaphoreType.DMA((9,)),
            pltpu.SemaphoreType.DMA((8,)),
            pltpu.SemaphoreType.DMA((8,)),
            pltpu.SemaphoreType.DMA((3,)),
        ],
        name="pose_solve",
        compiler_params=pltpu.CompilerParams(
            collective_id=0, has_side_effects=True, vmem_limit_bytes=48 * 2**20
        ),
    )(
        *(pltpu.with_memory_space_constraint(x, pltpu.HBM) for x in inputs)
    )
    out = jax.ShapeDtypeStruct((PARAMS, COLS), F)
    return pl.pallas_call(
        place, out_shape=(out, out), in_specs=[vmem], out_specs=(vmem, vmem), name="pose_place",
        compiler_params=pltpu.CompilerParams(vmem_limit_bytes=8 * 2**20),
    )(result)


def solution(mesh):
    in_specs = (
        P(BOTH, None, None), P(BOTH), P(BOTH, None), P(), P(), P(), P(), P(None, BOTH), P(None, BOTH),
    )
    out_specs = (P(None, BOTH), P(None, BOTH))
    return jax.shard_map(body, mesh=mesh, in_specs=in_specs, out_specs=out_specs, check_vma=False)
```
